256 devices in a mesh: ctx: 64 (over z, y, core), head: 4 (over x).
Axes of the slice: x: 4, y: 4, z: 8, core: 2. Of those that a mesh axis runs over, the one named last changes fastest.
Arguments:
- queries: bfloat16 [65536, 1024], P('ctx', 'head'), may hold values from -6 to 6
- key_rows: bfloat16 [65536, 128], P('ctx'), may hold values from -6 to 6
- value_rows: bfloat16 [65536, 128], P('ctx'), may hold values from -6 to 6
- out_grad: bfloat16 [65536, 1024], P('ctx', 'head'), may hold values from -6 to 6
- block_lists: int32 [512, 8], P('ctx'), may hold values from -1 to 511, as said below
Outputs:
- attended: bfloat16 [65536, 1024], P('ctx', 'head')
- query_grad: bfloat16 [65536, 1024], P('ctx', 'head')
- key_grad: bfloat16 [65536, 128], P(('ctx', 'head'))
- value_grad: bfloat16 [65536, 128], P(('ctx', 'head'))
The draws below stay inside these ranges and needn't reach their ends.
Inputs may be any that keep to these rules, and one draw needn't show every extreme that they name: `block_lists`: entry 0 of row b is the position block of row b's own tokens. Every other entry is -1 or a block lying wholly before it whose rows belong to another index of ctx; the blocks of one row are distinct. Over the 8 rows of one index of ctx, at most 1 entries name blocks of any one other index, and in every draw some index has exactly 1 entries on one other.
All inputs are finite; a program needn't handle non-finite values.
Results may differ from the reference program's by a relative error of at most 0.022.
Values may be sent and summed in bfloat16 or wider, within the bound.
A program may use at most 128 MiB of HBM per device.

```python
import math
import jax
import jax.numpy as jnp
from jax import lax

HD = 128
GROUP = 8
BLK = 128
SEL = 8
TOK_DEV = 1024
QB = 8
L = 65536
NB = 512
N_CTX = 64


def draw_queries(key, part):
    total = TOK_DEV * N_CTX
    base = jnp.clip(jax.random.normal(key, (total, GROUP * HD), jnp.float32), -6.0, 6.0)
    return base.astype(jnp.bfloat16)


def draw_key_rows(key, part):
    total = TOK_DEV * N_CTX
    base = jnp.clip(jax.random.normal(key, (total, HD), jnp.float32), -6.0, 6.0)
    return base.astype(jnp.bfloat16)


def draw_block_lists(key, part):
    dev_count = N_CTX
    half_blocks = TOK_DEV // (2 * BLK)
    dev_blocks = 2 * half_blocks
    extras = SEL - 1

    def one_device(device):
        dev_key = jax.random.fold_in(key, device)
        shuffled = jax.random.permutation(dev_key, dev_count - 1).astype(jnp.int32)
        others = shuffled + (shuffled >= device).astype(jnp.int32)
        local_idx = jnp.arange(dev_blocks, dtype=jnp.int32)
        early_half = local_idx < half_blocks
        own_block = jnp.where(early_half, device * half_blocks + local_idx, (2 * dev_count - 1 - device) * half_blocks + local_idx - half_blocks)
        entry_index = local_idx[:, None] * extras + jnp.arange(extras, dtype=jnp.int32)[None, :]
        owners = others[entry_index % (dev_count - 1)]
        picked = jax.random.randint(jax.random.fold_in(dev_key, 7), (dev_blocks, extras), 0, 2 * half_blocks)
        late_ok = owners > device
        span_count = jnp.where(early_half[:, None] | ~late_ok, half_blocks, 2 * half_blocks)
        offset = picked % span_count
        picked_block = jnp.where(offset < half_blocks, owners * half_blocks + offset, (2 * dev_count - 1 - owners) * half_blocks + offset - half_blocks)
        usable = ~early_half[:, None] | (owners < device)
        picked_block = jnp.where(usable, picked_block, -1)
        return jnp.concatenate([own_block[:, None], picked_block], axis=1).astype(jnp.int32)
    result_rows = jax.vmap(one_device)(jnp.arange(dev_count, dtype=jnp.int32))
    return result_rows.reshape(dev_count * dev_blocks, SEL)


def level_of(own_key, extent, cuts, low, high):
    gain = 1.0
    for position, shards_of in cuts:
        draws = jax.random.uniform(jax.random.fold_in(jax.random.fold_in(own_key, 6), position), (shards_of,), jnp.float32, low / len(cuts), high / len(cuts))
        gain = gain * jnp.repeat(jnp.exp(draws), extent[position] // shards_of).reshape((-1,) + (1,) * (len(extent) - 1 - position))
    return gain


def noise(key, shape, spread, bound, split=(), kind=jnp.bfloat16):
    array = spread * jax.random.normal(key, shape, jnp.float32)
    if split:
        array = array * level_of(key, shape, split, -0.22, 0.18)
    return jnp.clip(array, -bound, bound).astype(kind)


def setup_inputs(seed: int = 0) -> dict:
    keys = jax.random.split(jax.random.key(seed), 6)
    queries = draw_queries(jax.random.fold_in(keys[5], 71), 0)
    key_rows = draw_key_rows(jax.random.fold_in(keys[5], 71), 0)
    value_rows = noise(keys[2], (L, HD), 1.0, 6.0, ((0, 64),))
    out_grad = noise(keys[3], (L, GROUP * HD), 1.0, 6.0, ((0, 64), (1, 4)))
    block_lists = draw_block_lists(jax.random.fold_in(keys[5], 71), 0)
    return dict(queries=queries, key_rows=key_rows, value_rows=value_rows, out_grad=out_grad, block_lists=block_lists)


NEG_FILL = -1e+30
HIGHEST_PREC = lax.Precision.HIGHEST

def rounded(values):
    return lax.optimization_barrier(values.astype(jnp.bfloat16)).astype(jnp.float32)

def reference(queries, key_rows, value_rows, out_grad, block_lists):
    pair_count = N_CTX
    half_blocks = TOK_DEV // (2 * BLK)
    score_scale = 1.0 / math.sqrt(HD)
    key_tiles = key_rows.reshape(NB, BLK, HD).astype(jnp.float32)
    value_tiles = value_rows.reshape(NB, BLK, HD).astype(jnp.float32)
    query_tiles = queries.reshape(NB, BLK, GROUP, HD)
    grad_tiles = out_grad.reshape(NB, BLK, GROUP, HD)
    row_ids = jnp.arange(NB, dtype=jnp.int32)
    device = row_ids // QB
    within = row_ids % QB
    own_block = jnp.where(within < half_blocks, device * half_blocks + within, (2 * pair_count - 1 - device) * half_blocks + within - half_blocks).astype(jnp.int32)
    offsets = jnp.arange(BLK, dtype=jnp.int32)

    def per_block(carry, inputs):
        key_acc, value_acc = carry
        query_blk, grad_blk, list_row, own_pos = inputs
        usable = list_row >= 0
        safe_row = jnp.maximum(list_row, 0)
        stretch_idx = safe_row // half_blocks
        early_side = stretch_idx < pair_count
        owner_dev = jnp.where(early_side, stretch_idx, 2 * pair_count - 1 - stretch_idx)
        local_blk = safe_row % half_blocks + jnp.where(early_side, 0, half_blocks)
        stored = (owner_dev * QB + local_blk).astype(jnp.int32)
        keys_sel = key_tiles[stored]
        values_sel = value_tiles[stored]
        query_pos = own_pos * BLK + offsets
        key_pos = safe_row[:, None] * BLK + offsets[None, :]
        visible = usable[None, :, None] & (key_pos[None] <= query_pos[:, None, None])
        query_f = query_blk.astype(jnp.float32)
        grad_f = grad_blk.astype(jnp.float32)
        scores = jnp.einsum('ihd,sjd->hisj', query_f, keys_sel, precision=HIGHEST_PREC) * score_scale
        scores = jnp.where(visible[None], scores, NEG_FILL)
        row_max = lax.optimization_barrier(jnp.max(scores, axis=(2, 3), keepdims=True))
        weights = jnp.exp(scores - row_max)
        row_total = lax.optimization_barrier(jnp.sum(weights, axis=(2, 3), keepdims=True))
        summed = jnp.einsum('hisj,sjd->ihd', rounded(weights), values_sel, precision=HIGHEST_PREC)
        attended = (summed / jnp.transpose(row_total[:, :, 0, 0])[:, :, None]).astype(jnp.bfloat16)
        log_total = row_max + jnp.log(row_total)
        probability = jnp.exp(scores - log_total)
        row_delta = lax.optimization_barrier(jnp.sum(grad_f * attended.astype(jnp.float32), axis=2))
        grad_p = jnp.einsum('ihd,sjd->hisj', grad_f, values_sel, precision=HIGHEST_PREC)
        grad_s = rounded(probability * (grad_p - jnp.transpose(row_delta)[:, :, None, None]))
        query_grad = (jnp.einsum('hisj,sjd->ihd', grad_s, keys_sel, precision=HIGHEST_PREC) * score_scale).astype(jnp.bfloat16)
        key_part = jnp.einsum('hisj,ihd->sjd', grad_s, query_f, precision=HIGHEST_PREC) * score_scale
        value_part = jnp.einsum('hisj,ihd->sjd', rounded(probability), grad_f, precision=HIGHEST_PREC)
        target = jnp.where(usable, stored, NB).astype(jnp.int32)
        key_acc = key_acc.at[target].add(key_part, mode='drop')
        value_acc = value_acc.at[target].add(value_part, mode='drop')
        return ((key_acc, value_acc), (attended, query_grad))
    start = jnp.zeros((NB, BLK, HD), jnp.float32)
    (key_acc, value_acc), (attended, query_grad) = lax.scan(per_block, (start, start), (query_tiles, grad_tiles, block_lists, own_block))
    return (attended.reshape(NB * BLK, GROUP * HD), query_grad.reshape(NB * BLK, GROUP * HD), key_acc.reshape(NB * BLK, HD).astype(jnp.bfloat16), value_acc.reshape(NB * BLK, HD).astype(jnp.bfloat16))
```

```python
import math

import jax
import jax.numpy as jnp
from jax import lax
from jax.sharding import PartitionSpec as P

HD = 128
BLK = 128
SEL = 8
QB = 8


NEG_FILL = -1e30


def block_home(block, half_blocks, pair_count):
    stretch_idx = block // half_blocks
    early_side = stretch_idx < pair_count
    owner_dev = jnp.where(early_side, stretch_idx, 2 * pair_count - 1 - stretch_idx)
    local_blk = block % half_blocks + jnp.where(early_side, 0, half_blocks)
    return (owner_dev, local_blk)


def entry_slots(list_rows, half_blocks, pair_count):
    extras = list_rows[:, 1:].reshape(-1)
    usable = extras >= 0
    owner_dev, local_blk = block_home(jnp.maximum(extras, 0), half_blocks, pair_count)
    onehot_own = (
        (owner_dev[:, None] == jnp.arange(pair_count, dtype=jnp.int32)[None, :]) & usable[:, None]
    ).astype(jnp.int32)
    running = jnp.cumsum(onehot_own, axis=0)
    rank_in = jnp.sum(onehot_own * running, axis=1) - 1
    return (owner_dev, local_blk, rank_in, usable)


def on_device(queries, key_rows, value_rows, out_grad, block_lists):
    pair_count = lax.axis_size("ctx")
    half_blocks = QB // 2
    capacity = (QB * (SEL - 1) + pair_count - 2) // (pair_count - 1)
    total_slots = pair_count * capacity
    device = lax.axis_index("ctx")
    score_scale = 1.0 / math.sqrt(HD)
    owner_dev, local_blk, rank_in, usable = entry_slots(block_lists, half_blocks, pair_count)
    slot_idx = jnp.where(usable, owner_dev * capacity + rank_in, total_slots)
    req_table = (
        jnp.full((total_slots + 1,), -1, jnp.int32).at[slot_idx].set(local_blk)[:total_slots]
    )
    requested = lax.all_to_all(
        req_table.reshape(pair_count, capacity), "ctx", split_axis=0, concat_axis=0, tiled=True
    )
    head_count = lax.axis_size("head")
    head_idx = lax.axis_index("head")
    part_rows = 2 * BLK // head_count
    kv_blocks = jnp.stack([key_rows.reshape(QB, BLK, HD), value_rows.reshape(QB, BLK, HD)], axis=1)
    kv_parts = kv_blocks.reshape(QB, head_count, part_rows, HD)
    my_part = lax.dynamic_index_in_dim(kv_parts, head_idx, axis=1, keepdims=False)
    send_parts = my_part[jnp.maximum(requested, 0)]
    fetched_part = lax.all_to_all(send_parts, "ctx", split_axis=0, concat_axis=0, tiled=True)
    fetched = lax.all_gather(fetched_part, "head", axis=2, tiled=False)
    kv_table = jnp.concatenate([kv_blocks, fetched.reshape(total_slots, 2, BLK, HD)], axis=0)
    local_ids = jnp.arange(QB, dtype=jnp.int32)
    remote_idx = jnp.where(usable, QB + slot_idx, 0).reshape(QB, SEL - 1)
    entry_idx = jnp.concatenate([local_ids[:, None], remote_idx], axis=1)
    kv_tiles = kv_table[entry_idx]
    key_tile = kv_tiles[:, :, 0]
    value_tile = kv_tiles[:, :, 1]
    own_block = jnp.where(
        local_ids < half_blocks,
        device * half_blocks + local_ids,
        (2 * pair_count - 1 - device) * half_blocks + local_ids - half_blocks,
    )
    offsets = jnp.arange(BLK, dtype=jnp.int32)
    query_pos = own_block[:, None] * BLK + offsets[None, :]
    key_pos = jnp.maximum(block_lists, 0)[:, :, None] * BLK + offsets[None, None, :]
    visible = (block_lists >= 0)[:, None, :, None] & (
        key_pos[:, None, :, :] <= query_pos[:, :, None, None]
    )
    heads_here = queries.shape[1] // HD
    q_blocks = queries.reshape(QB, BLK, heads_here, HD)
    g_blocks = out_grad.reshape(QB, BLK, heads_here, HD)
    scores = (
        jnp.einsum("qihd,qsjd->qhisj", q_blocks, key_tile, preferred_element_type=jnp.float32)
        * score_scale
    )
    scores = jnp.where(visible[:, None], scores, NEG_FILL)
    row_max = jnp.max(scores, axis=(3, 4), keepdims=True)
    weights = jnp.exp(scores - row_max)
    row_total = jnp.sum(weights, axis=(3, 4), keepdims=True)
    summed = jnp.einsum(
        "qhisj,qsjd->qihd",
        weights.astype(jnp.bfloat16),
        value_tile,
        preferred_element_type=jnp.float32,
    )
    attended = (summed / jnp.transpose(row_total[..., 0, 0], (0, 2, 1))[..., None]).astype(
        jnp.bfloat16
    )
    log_total = row_max + jnp.log(row_total)
    probability = jnp.exp(scores - log_total)
    row_delta = jnp.sum(g_blocks.astype(jnp.float32) * attended.astype(jnp.float32), axis=3)
    grad_p = jnp.einsum(
        "qihd,qsjd->qhisj", g_blocks, value_tile, preferred_element_type=jnp.float32
    )
    grad_s = (probability * (grad_p - jnp.transpose(row_delta, (0, 2, 1))[..., None, None])).astype(
        jnp.bfloat16
    )
    query_grad = (
        jnp.einsum("qhisj,qsjd->qihd", grad_s, key_tile, preferred_element_type=jnp.float32)
        * score_scale
    ).astype(jnp.bfloat16)
    key_part = (
        jnp.einsum("qhisj,qihd->qsjd", grad_s, q_blocks, preferred_element_type=jnp.float32)
        * score_scale
    )
    value_part = jnp.einsum(
        "qhisj,qihd->qsjd",
        probability.astype(jnp.bfloat16),
        g_blocks,
        preferred_element_type=jnp.float32,
    )
    grad_tiles = jnp.stack([key_part, value_part], axis=2)
    entry_count = QB * (SEL - 1)
    slot_entry = (
        jnp.full((total_slots + 1,), entry_count, jnp.int32)
        .at[slot_idx]
        .set(jnp.arange(entry_count, dtype=jnp.int32))[:total_slots]
    )
    remote_tiles = jnp.concatenate(
        [grad_tiles[:, 1:].reshape(entry_count, 2, BLK, HD), jnp.zeros((1, 2, BLK, HD), jnp.float32)],
        axis=0,
    )
    remote_parts = jnp.moveaxis(remote_tiles.reshape(entry_count + 1, head_count, part_rows, HD), 1, 0)
    outgoing = remote_parts[:, slot_entry].astype(jnp.bfloat16)
    outgoing_part = lax.psum_scatter(
        outgoing.reshape(head_count * total_slots * part_rows, HD), "head", scatter_dimension=0, tiled=True
    )
    returned = lax.all_to_all(
        outgoing_part.reshape(pair_count, capacity, part_rows, HD),
        "ctx",
        split_axis=0,
        concat_axis=0,
        tiled=True,
    ).astype(jnp.float32)
    target = jnp.where(requested >= 0, requested, QB).reshape(-1)
    returned_sum = (
        jnp.zeros((QB + 1, part_rows, HD), jnp.float32)
        .at[target]
        .add(returned.reshape(-1, part_rows, HD))[:QB]
    )
    own_parts = grad_tiles[:, 0].reshape(QB, head_count, part_rows, HD)
    mine = (jnp.arange(head_count, dtype=jnp.int32) == head_idx)[None, :, None, None]
    own_parts = own_parts + jnp.where(mine, returned_sum[:, None], 0.0)
    combined = jnp.transpose(own_parts.reshape(QB, 2, BLK, HD), (1, 0, 2, 3)).reshape(2, QB * BLK, HD)
    reduced = lax.psum_scatter(
        combined.astype(jnp.bfloat16), "head", scatter_dimension=1, tiled=True
    ).astype(jnp.float32)
    return (
        attended.reshape(QB * BLK, heads_here * HD),
        query_grad.reshape(QB * BLK, heads_here * HD),
        reduced[0].astype(jnp.bfloat16),
        reduced[1].astype(jnp.bfloat16),
    )


def solution(mesh):
    return jax.shard_map(
        on_device,
        mesh=mesh,
        in_specs=(
            P("ctx", "head"),
            P("ctx", None),
            P("ctx", None),
            P("ctx", "head"),
            P("ctx", None),
        ),
        out_specs=(
            P("ctx", "head"),
            P("ctx", "head"),
            P(("ctx", "head"), None),
            P(("ctx", "head"), None),
        ),
        check_vma=False,
    )
```

```python
import math

import jax
import jax.numpy as jnp
from jax import lax
from jax.sharding import PartitionSpec as P

HD = 128
BLK = 128
SEL = 8
QB = 8


NEG_FILL = -1e30


def block_home(block, half_blocks, pair_count):
    stretch_idx = block // half_blocks
    early_side = stretch_idx < pair_count
    owner_dev = jnp.where(early_side, stretch_idx, 2 * pair_count - 1 - stretch_idx)
    local_blk = block % half_blocks + jnp.where(early_side, 0, half_blocks)
    return (owner_dev, local_blk)


def entry_slots(list_rows, half_blocks, pair_count):
    extras = list_rows[:, 1:].reshape(-1)
    usable = extras >= 0
    owner_dev, local_blk = block_home(jnp.maximum(extras, 0), half_blocks, pair_count)
    onehot_own = (
        (owner_dev[:, None] == jnp.arange(pair_count, dtype=jnp.int32)[None, :]) & usable[:, None]
    ).astype(jnp.int32)
    running = jnp.cumsum(onehot_own, axis=0)
    rank_in = jnp.sum(onehot_own * running, axis=1) - 1
    return (owner_dev, local_blk, rank_in, usable)


def head_shift(x, shift, count):
    return lax.ppermute(x, "head", [(j, (j + shift) % count) for j in range(count)])


def head_gather(part, head_idx, count):
    by_shift = jnp.stack([part] + [head_shift(part, k, count) for k in range(1, count)])
    order = (head_idx - jnp.arange(count, dtype=jnp.int32)) % count
    return by_shift[order]


def head_reduce(parts, head_idx, count):
    total = lax.dynamic_index_in_dim(parts, head_idx, axis=0, keepdims=False).astype(jnp.float32)
    for k in range(1, count):
        piece = lax.dynamic_index_in_dim(parts, (head_idx + k) % count, axis=0, keepdims=False)
        total = total + head_shift(piece, k, count).astype(jnp.float32)
    return total


def on_device(queries, key_rows, value_rows, out_grad, block_lists):
    pair_count = lax.axis_size("ctx")
    half_blocks = QB // 2
    capacity = (QB * (SEL - 1) + pair_count - 2) // (pair_count - 1)
    total_slots = pair_count * capacity
    device = lax.axis_index("ctx")
    score_scale = 1.0 / math.sqrt(HD)
    owner_dev, local_blk, rank_in, usable = entry_slots(block_lists, half_blocks, pair_count)
    slot_idx = jnp.where(usable, owner_dev * capacity + rank_in, total_slots)
    req_table = (
        jnp.full((total_slots + 1,), -1, jnp.int32).at[slot_idx].set(local_blk)[:total_slots]
    )
    requested = lax.all_to_all(
        req_table.reshape(pair_count, capacity), "ctx", split_axis=0, concat_axis=0, tiled=True
    )
    head_count = lax.axis_size("head")
    head_idx = lax.axis_index("head")
    part_rows = 2 * BLK // head_count
    kv_blocks = jnp.stack([key_rows.reshape(QB, BLK, HD), value_rows.reshape(QB, BLK, HD)], axis=1)
    kv_parts = kv_blocks.reshape(QB, head_count, part_rows, HD)
    my_part = lax.dynamic_index_in_dim(kv_parts, head_idx, axis=1, keepdims=False)
    send_parts = my_part[jnp.maximum(requested, 0)]
    fetched_part = lax.all_to_all(send_parts, "ctx", split_axis=0, concat_axis=0, tiled=True)
    fetched = jnp.moveaxis(head_gather(fetched_part, head_idx, head_count), 0, 2)
    kv_table = jnp.concatenate([kv_blocks, fetched.reshape(total_slots, 2, BLK, HD)], axis=0)
    local_ids = jnp.arange(QB, dtype=jnp.int32)
    remote_idx = jnp.where(usable, QB + slot_idx, 0).reshape(QB, SEL - 1)
    entry_idx = jnp.concatenate([local_ids[:, None], remote_idx], axis=1)
    kv_tiles = kv_table[entry_idx]
    key_tile = kv_tiles[:, :, 0]
    value_tile = kv_tiles[:, :, 1]
    own_block = jnp.where(
        local_ids < half_blocks,
        device * half_blocks + local_ids,
        (2 * pair_count - 1 - device) * half_blocks + local_ids - half_blocks,
    )
    offsets = jnp.arange(BLK, dtype=jnp.int32)
    query_pos = own_block[:, None] * BLK + offsets[None, :]
    key_pos = jnp.maximum(block_lists, 0)[:, :, None] * BLK + offsets[None, None, :]
    visible = (block_lists >= 0)[:, None, :, None] & (
        key_pos[:, None, :, :] <= query_pos[:, :, None, None]
    )
    heads_here = queries.shape[1] // HD
    q_blocks = queries.reshape(QB, BLK, heads_here, HD)
    g_blocks = out_grad.reshape(QB, BLK, heads_here, HD)
    scores = (
        jnp.einsum("qihd,qsjd->qhisj", q_blocks, key_tile, preferred_element_type=jnp.float32)
        * score_scale
    )
    scores = jnp.where(visible[:, None], scores, NEG_FILL)
    row_max = jnp.max(scores, axis=(3, 4), keepdims=True)
    weights = jnp.exp(scores - row_max)
    row_total = jnp.sum(weights, axis=(3, 4), keepdims=True)
    summed = jnp.einsum(
        "qhisj,qsjd->qihd",
        weights.astype(jnp.bfloat16),
        value_tile,
        preferred_element_type=jnp.float32,
    )
    attended = (summed / jnp.transpose(row_total[..., 0, 0], (0, 2, 1))[..., None]).astype(
        jnp.bfloat16
    )
    log_total = row_max + jnp.log(row_total)
    probability = jnp.exp(scores - log_total)
    row_delta = jnp.sum(g_blocks.astype(jnp.float32) * attended.astype(jnp.float32), axis=3)
    grad_p = jnp.einsum(
        "qihd,qsjd->qhisj", g_blocks, value_tile, preferred_element_type=jnp.float32
    )
    grad_s = (probability * (grad_p - jnp.transpose(row_delta, (0, 2, 1))[..., None, None])).astype(
        jnp.bfloat16
    )
    query_grad = (
        jnp.einsum("qhisj,qsjd->qihd", grad_s, key_tile, preferred_element_type=jnp.float32)
        * score_scale
    ).astype(jnp.bfloat16)
    key_part = (
        jnp.einsum("qhisj,qihd->qsjd", grad_s, q_blocks, preferred_element_type=jnp.float32)
        * score_scale
    )
    value_part = jnp.einsum(
        "qhisj,qihd->qsjd",
        probability.astype(jnp.bfloat16),
        g_blocks,
        preferred_element_type=jnp.float32,
    )
    grad_tiles = jnp.stack([key_part, value_part], axis=2)
    entry_count = QB * (SEL - 1)
    slot_entry = (
        jnp.full((total_slots + 1,), entry_count, jnp.int32)
        .at[slot_idx]
        .set(jnp.arange(entry_count, dtype=jnp.int32))[:total_slots]
    )
    remote_tiles = jnp.concatenate(
        [grad_tiles[:, 1:].reshape(entry_count, 2, BLK, HD), jnp.zeros((1, 2, BLK, HD), jnp.float32)],
        axis=0,
    )
    remote_parts = jnp.moveaxis(remote_tiles.reshape(entry_count + 1, head_count, part_rows, HD), 1, 0)
    outgoing = remote_parts[:, slot_entry].astype(jnp.bfloat16)
    outgoing_part = head_reduce(outgoing, head_idx, head_count).astype(jnp.bfloat16)
    returned = lax.all_to_all(
        outgoing_part.reshape(pair_count, capacity, part_rows, HD),
        "ctx",
        split_axis=0,
        concat_axis=0,
        tiled=True,
    ).astype(jnp.float32)
    target = jnp.where(requested >= 0, requested, QB).reshape(-1)
    returned_sum = (
        jnp.zeros((QB + 1, part_rows, HD), jnp.float32)
        .at[target]
        .add(returned.reshape(-1, part_rows, HD))[:QB]
    )
    own_parts = grad_tiles[:, 0].reshape(QB, head_count, part_rows, HD)
    mine = (jnp.arange(head_count, dtype=jnp.int32) == head_idx)[None, :, None, None]
    own_parts = own_parts + jnp.where(mine, returned_sum[:, None], 0.0)
    combined = jnp.transpose(own_parts.reshape(head_count, QB // head_count, 2, BLK, HD), (0, 2, 1, 3, 4))
    reduced = head_reduce(combined.astype(jnp.bfloat16), head_idx, head_count).reshape(2, -1, HD)
    return (
        attended.reshape(QB * BLK, heads_here * HD),
        query_grad.reshape(QB * BLK, heads_here * HD),
        reduced[0].astype(jnp.bfloat16),
        reduced[1].astype(jnp.bfloat16),
    )


def solution(mesh):
    return jax.shard_map(
        on_device,
        mesh=mesh,
        in_specs=(
            P("ctx", "head"),
            P("ctx", None),
            P("ctx", None),
            P("ctx", "head"),
            P("ctx", None),
        ),
        out_specs=(
            P("ctx", "head"),
            P("ctx", "head"),
            P(("ctx", "head"), None),
            P(("ctx", "head"), None),
        ),
        check_vma=False,
    )
```

```python
import math

import jax
import jax.numpy as jnp
from jax import lax
from jax.sharding import PartitionSpec as P

HD = 128
BLK = 128
SEL = 8
QB = 8


NEG_FILL = -1e30


def block_home(block, half_blocks, pair_count):
    stretch_idx = block // half_blocks
    early_side = stretch_idx < pair_count
    owner_dev = jnp.where(early_side, stretch_idx, 2 * pair_count - 1 - stretch_idx)
    local_blk = block % half_blocks + jnp.where(early_side, 0, half_blocks)
    return (owner_dev, local_blk)


def entry_slots(list_rows, half_blocks, pair_count):
    extras = list_rows[:, 1:].reshape(-1)
    usable = extras >= 0
    owner_dev, local_blk = block_home(jnp.maximum(extras, 0), half_blocks, pair_count)
    onehot_own = (
        (owner_dev[:, None] == jnp.arange(pair_count, dtype=jnp.int32)[None, :]) & usable[:, None]
    ).astype(jnp.int32)
    running = jnp.cumsum(onehot_own, axis=0)
    rank_in = jnp.sum(onehot_own * running, axis=1) - 1
    return (owner_dev, local_blk, rank_in, usable)


def rows_to_heads_split(x, head_count):
    rows, cols = x.shape
    parts = lax.all_to_all(
        x.reshape(head_count, rows // head_count, cols), "head", split_axis=0, concat_axis=0, tiled=True
    )
    return jnp.transpose(parts, (1, 0, 2)).reshape(rows // head_count, head_count * cols)


def heads_to_rows_split(y, head_count):
    rows, cols = y.shape
    parts = jnp.transpose(y.reshape(rows, head_count, cols // head_count), (1, 0, 2))
    parts = lax.all_to_all(parts, "head", split_axis=0, concat_axis=0, tiled=True)
    return parts.reshape(rows * head_count, cols // head_count)


def on_device(queries, key_rows, value_rows, out_grad, block_lists):
    pair_count = lax.axis_size("ctx")
    head_count = lax.axis_size("head")
    half_blocks = QB // 2
    capacity = (QB * (SEL - 1) + pair_count - 2) // (pair_count - 1)
    total_slots = pair_count * capacity
    device = lax.axis_index("ctx")
    head_idx = lax.axis_index("head")
    score_scale = 1.0 / math.sqrt(HD)
    rows_here = QB // head_count
    extras = SEL - 1
    entry_count = QB * extras
    my_entries = rows_here * extras
    part_rows = 2 * BLK // head_count
    owner_dev, local_blk, rank_in, usable = entry_slots(block_lists, half_blocks, pair_count)
    slot_idx = jnp.where(usable, owner_dev * capacity + rank_in, total_slots)
    req_table = (
        jnp.full((total_slots + 1,), -1, jnp.int32).at[slot_idx].set(local_blk)[:total_slots]
    )
    requested = lax.all_to_all(
        req_table.reshape(pair_count, capacity), "ctx", split_axis=0, concat_axis=0, tiled=True
    )
    q_rows = rows_to_heads_split(queries, head_count)
    g_rows = rows_to_heads_split(out_grad, head_count)
    heads_all = q_rows.shape[1] // HD
    kv_blocks = jnp.stack([key_rows.reshape(QB, BLK, HD), value_rows.reshape(QB, BLK, HD)], axis=1)
    kv_parts = kv_blocks.reshape(QB, head_count, part_rows, HD)
    my_part = lax.dynamic_index_in_dim(kv_parts, head_idx, axis=1, keepdims=False)
    send_parts = my_part[jnp.maximum(requested, 0)]
    fetched_part = lax.all_to_all(send_parts, "ctx", split_axis=0, concat_axis=0, tiled=True).reshape(
        total_slots, part_rows, HD
    )
    entry_slot = jnp.where(usable, slot_idx, 0).reshape(head_count, my_entries)
    share = fetched_part[entry_slot]
    got = lax.all_to_all(share, "head", split_axis=0, concat_axis=0, tiled=True)
    remote_kv = jnp.transpose(got, (1, 0, 2, 3)).reshape(rows_here, extras, 2, BLK, HD)
    first_row = head_idx * rows_here
    own_kv = lax.dynamic_slice_in_dim(kv_blocks, first_row, rows_here, axis=0)
    kv_tiles = jnp.concatenate([own_kv[:, None], remote_kv], axis=1)
    key_tile = kv_tiles[:, :, 0]
    value_tile = kv_tiles[:, :, 1]
    my_lists = lax.dynamic_slice_in_dim(block_lists, first_row, rows_here, axis=0)
    local_ids = first_row + jnp.arange(rows_here, dtype=jnp.int32)
    own_block = jnp.where(
        local_ids < half_blocks,
        device * half_blocks + local_ids,
        (2 * pair_count - 1 - device) * half_blocks + local_ids - half_blocks,
    )
    offsets = jnp.arange(BLK, dtype=jnp.int32)
    query_pos = own_block[:, None] * BLK + offsets[None, :]
    key_pos = jnp.maximum(my_lists, 0)[:, :, None] * BLK + offsets[None, None, :]
    visible = (my_lists >= 0)[:, None, :, None] & (
        key_pos[:, None, :, :] <= query_pos[:, :, None, None]
    )
    q_blocks = q_rows.reshape(rows_here, BLK, heads_all, HD)
    g_blocks = g_rows.reshape(rows_here, BLK, heads_all, HD)
    scores = (
        jnp.einsum("qihd,qsjd->qhisj", q_blocks, key_tile, preferred_element_type=jnp.float32)
        * score_scale
    )
    scores = jnp.where(visible[:, None], scores, NEG_FILL)
    row_max = jnp.max(scores, axis=(3, 4), keepdims=True)
    weights = jnp.exp(scores - row_max)
    row_total = jnp.sum(weights, axis=(3, 4), keepdims=True)
    summed = jnp.einsum(
        "qhisj,qsjd->qihd",
        weights.astype(jnp.bfloat16),
        value_tile,
        preferred_element_type=jnp.float32,
    )
    attended = (summed / jnp.transpose(row_total[..., 0, 0], (0, 2, 1))[..., None]).astype(
        jnp.bfloat16
    )
    log_total = row_max + jnp.log(row_total)
    probability = jnp.exp(scores - log_total)
    row_delta = jnp.sum(g_blocks.astype(jnp.float32) * attended.astype(jnp.float32), axis=3)
    grad_p = jnp.einsum(
        "qihd,qsjd->qhisj", g_blocks, value_tile, preferred_element_type=jnp.float32
    )
    grad_s = (probability * (grad_p - jnp.transpose(row_delta, (0, 2, 1))[..., None, None])).astype(
        jnp.bfloat16
    )
    query_grad = (
        jnp.einsum("qhisj,qsjd->qihd", grad_s, key_tile, preferred_element_type=jnp.float32)
        * score_scale
    ).astype(jnp.bfloat16)
    key_part = (
        jnp.einsum("qhisj,qihd->qsjd", grad_s, q_blocks, preferred_element_type=jnp.float32)
        * score_scale
    )
    value_part = jnp.einsum(
        "qhisj,qihd->qsjd",
        probability.astype(jnp.bfloat16),
        g_blocks,
        preferred_element_type=jnp.float32,
    )
    grad_tiles = jnp.stack([key_part, value_part], axis=2)
    remote_grad = grad_tiles[:, 1:].astype(jnp.bfloat16).reshape(my_entries, head_count, part_rows, HD)
    back = lax.all_to_all(
        jnp.transpose(remote_grad, (1, 0, 2, 3)), "head", split_axis=0, concat_axis=0, tiled=True
    ).reshape(entry_count, part_rows, HD)
    slot_entry = (
        jnp.full((total_slots + 1,), entry_count, jnp.int32)
        .at[slot_idx]
        .set(jnp.arange(entry_count, dtype=jnp.int32))[:total_slots]
    )
    back = jnp.concatenate([back, jnp.zeros((1, part_rows, HD), back.dtype)], axis=0)
    outgoing_part = back[slot_entry]
    returned = lax.all_to_all(
        outgoing_part.reshape(pair_count, capacity, part_rows, HD),
        "ctx",
        split_axis=0,
        concat_axis=0,
        tiled=True,
    ).astype(jnp.float32)
    target = jnp.where(requested >= 0, requested, QB).reshape(-1)
    returned_sum = (
        jnp.zeros((QB + 1, part_rows, HD), jnp.float32)
        .at[target]
        .add(returned.reshape(-1, part_rows, HD))[:QB]
    )
    routed = lax.all_to_all(
        returned_sum.reshape(head_count, rows_here, part_rows, HD),
        "head",
        split_axis=0,
        concat_axis=0,
        tiled=True,
    )
    routed = jnp.transpose(routed, (1, 0, 2, 3)).reshape(rows_here, 2, BLK, HD)
    final = grad_tiles[:, 0] + routed
    attended_out = heads_to_rows_split(attended.reshape(rows_here * BLK, heads_all * HD), head_count)
    query_grad_out = heads_to_rows_split(query_grad.reshape(rows_here * BLK, heads_all * HD), head_count)
    return (
        attended_out,
        query_grad_out,
        final[:, 0].reshape(rows_here * BLK, HD).astype(jnp.bfloat16),
        final[:, 1].reshape(rows_here * BLK, HD).astype(jnp.bfloat16),
    )

def solution(mesh):
    return jax.shard_map(
        on_device,
        mesh=mesh,
        in_specs=(
            P("ctx", "head"),
            P("ctx", None),
            P("ctx", None),
            P("ctx", "head"),
            P("ctx", None),
        ),
        out_specs=(
            P("ctx", "head"),
            P("ctx", "head"),
            P(("ctx", "head"), None),
            P(("ctx", "head"), None),
        ),
        check_vma=False,
    )
```

```python
import math

import jax
import jax.numpy as jnp
from jax import lax
from jax.sharding import PartitionSpec as P

HD = 128
BLK = 128
SEL = 8
QB = 8


NEG_FILL = -1e30


def block_home(block, half_blocks, pair_count):
    stretch_idx = block // half_blocks
    early_side = stretch_idx < pair_count
    owner_dev = jnp.where(early_side, stretch_idx, 2 * pair_count - 1 - stretch_idx)
    local_blk = block % half_blocks + jnp.where(early_side, 0, half_blocks)
    return (owner_dev, local_blk)


def entry_slots(list_rows, half_blocks, pair_count):
    extras = list_rows[:, 1:].reshape(-1)
    usable = extras >= 0
    owner_dev, local_blk = block_home(jnp.maximum(extras, 0), half_blocks, pair_count)
    onehot_own = (
        (owner_dev[:, None] == jnp.arange(pair_count, dtype=jnp.int32)[None, :]) & usable[:, None]
    ).astype(jnp.int32)
    running = jnp.cumsum(onehot_own, axis=0)
    rank_in = jnp.sum(onehot_own * running, axis=1) - 1
    return (owner_dev, local_blk, rank_in, usable)


def on_device(queries, key_rows, value_rows, out_grad, block_lists):
    pair_count = lax.axis_size("ctx")
    head_count = lax.axis_size("head")
    half_blocks = QB // 2
    capacity = (QB * (SEL - 1) + pair_count - 2) // (pair_count - 1)
    total_slots = pair_count * capacity
    device = lax.axis_index("ctx")
    head_idx = lax.axis_index("head")
    score_scale = 1.0 / math.sqrt(HD)
    rows_here = QB // head_count
    extras = SEL - 1
    entry_count = QB * extras
    my_entries = rows_here * extras
    part_rows = 2 * BLK // head_count
    owner_dev, local_blk, rank_in, usable = entry_slots(block_lists, half_blocks, pair_count)
    slot_idx = jnp.where(usable, owner_dev * capacity + rank_in, total_slots)
    req_table = (
        jnp.full((total_slots + 1,), -1, jnp.int32).at[slot_idx].set(local_blk)[:total_slots]
    )
    requested = lax.all_to_all(
        req_table.reshape(pair_count, capacity), "ctx", split_axis=0, concat_axis=0, tiled=True
    )
    rows_in, cols_in = queries.shape
    inputs_split = jnp.stack(
        [
            queries.reshape(head_count, rows_in // head_count, cols_in),
            out_grad.reshape(head_count, rows_in // head_count, cols_in),
        ],
        axis=1,
    )
    inputs_rows = lax.all_to_all(inputs_split, "head", split_axis=0, concat_axis=0, tiled=True)
    inputs_rows = jnp.transpose(inputs_rows, (1, 2, 0, 3)).reshape(2, rows_in // head_count, head_count * cols_in)
    q_rows = inputs_rows[0]
    g_rows = inputs_rows[1]
    heads_all = q_rows.shape[1] // HD
    kv_blocks = jnp.stack([key_rows.reshape(QB, BLK, HD), value_rows.reshape(QB, BLK, HD)], axis=1)
    kv_parts = kv_blocks.reshape(QB, head_count, part_rows, HD)
    my_part = lax.dynamic_index_in_dim(kv_parts, head_idx, axis=1, keepdims=False)
    send_parts = my_part[jnp.maximum(requested, 0)]
    fetched_part = lax.all_to_all(send_parts, "ctx", split_axis=0, concat_axis=0, tiled=True).reshape(
        total_slots, part_rows, HD
    )
    entry_slot = jnp.where(usable, slot_idx, 0).reshape(head_count, my_entries)
    share = fetched_part[entry_slot]
    got = lax.all_to_all(share, "head", split_axis=0, concat_axis=0, tiled=True)
    remote_kv = jnp.transpose(got, (1, 0, 2, 3)).reshape(rows_here, extras, 2, BLK, HD)
    first_row = head_idx * rows_here
    own_kv = lax.dynamic_slice_in_dim(kv_blocks, first_row, rows_here, axis=0)
    kv_tiles = jnp.concatenate([own_kv[:, None], remote_kv], axis=1)
    key_tile = kv_tiles[:, :, 0]
    value_tile = kv_tiles[:, :, 1]
    my_lists = lax.dynamic_slice_in_dim(block_lists, first_row, rows_here, axis=0)
    local_ids = first_row + jnp.arange(rows_here, dtype=jnp.int32)
    own_block = jnp.where(
        local_ids < half_blocks,
        device * half_blocks + local_ids,
        (2 * pair_count - 1 - device) * half_blocks + local_ids - half_blocks,
    )
    offsets = jnp.arange(BLK, dtype=jnp.int32)
    query_pos = own_block[:, None] * BLK + offsets[None, :]
    key_pos = jnp.maximum(my_lists, 0)[:, :, None] * BLK + offsets[None, None, :]
    visible = (my_lists >= 0)[:, None, :, None] & (
        key_pos[:, None, :, :] <= query_pos[:, :, None, None]
    )
    q_blocks = q_rows.reshape(rows_here, BLK, heads_all, HD)
    g_blocks = g_rows.reshape(rows_here, BLK, heads_all, HD)
    scores = (
        jnp.einsum("qihd,qsjd->qhisj", q_blocks, key_tile, preferred_element_type=jnp.float32)
        * score_scale
    )
    scores = jnp.where(visible[:, None], scores, NEG_FILL)
    row_max = jnp.max(scores, axis=(3, 4), keepdims=True)
    weights = jnp.exp(scores - row_max)
    row_total = jnp.sum(weights, axis=(3, 4), keepdims=True)
    summed = jnp.einsum(
        "qhisj,qsjd->qihd",
        weights.astype(jnp.bfloat16),
        value_tile,
        preferred_element_type=jnp.float32,
    )
    attended = (summed / jnp.transpose(row_total[..., 0, 0], (0, 2, 1))[..., None]).astype(
        jnp.bfloat16
    )
    log_total = row_max + jnp.log(row_total)
    probability = jnp.exp(scores - log_total)
    row_delta = jnp.sum(g_blocks.astype(jnp.float32) * attended.astype(jnp.float32), axis=3)
    grad_p = jnp.einsum(
        "qihd,qsjd->qhisj", g_blocks, value_tile, preferred_element_type=jnp.float32
    )
    grad_s = (probability * (grad_p - jnp.transpose(row_delta, (0, 2, 1))[..., None, None])).astype(
        jnp.bfloat16
    )
    query_grad = (
        jnp.einsum("qhisj,qsjd->qihd", grad_s, key_tile, preferred_element_type=jnp.float32)
        * score_scale
    ).astype(jnp.bfloat16)
    key_part = (
        jnp.einsum("qhisj,qihd->qsjd", grad_s, q_blocks, preferred_element_type=jnp.float32)
        * score_scale
    )
    value_part = jnp.einsum(
        "qhisj,qihd->qsjd",
        probability.astype(jnp.bfloat16),
        g_blocks,
        preferred_element_type=jnp.float32,
    )
    grad_tiles = jnp.stack([key_part, value_part], axis=2)
    remote_grad = grad_tiles[:, 1:].astype(jnp.bfloat16).reshape(my_entries, head_count, part_rows, HD)
    out_rows = rows_here * BLK
    out_cols = heads_all * HD // head_count
    outputs_split = jnp.transpose(
        jnp.stack([attended, query_grad]).reshape(2, out_rows, head_count, out_cols), (2, 0, 1, 3)
    )
    merged = jnp.concatenate(
        [
            outputs_split.reshape(head_count, -1),
            jnp.transpose(remote_grad, (1, 0, 2, 3)).reshape(head_count, -1),
        ],
        axis=1,
    )
    merged = lax.all_to_all(merged, "head", split_axis=0, concat_axis=0, tiled=True)
    outputs_rows = merged[:, : 2 * out_rows * out_cols].reshape(head_count, 2, out_rows, out_cols)
    outputs_rows = jnp.transpose(outputs_rows, (1, 0, 2, 3)).reshape(2, head_count * out_rows, out_cols)
    back = merged[:, 2 * out_rows * out_cols :].reshape(entry_count, part_rows, HD)
    slot_entry = (
        jnp.full((total_slots + 1,), entry_count, jnp.int32)
        .at[slot_idx]
        .set(jnp.arange(entry_count, dtype=jnp.int32))[:total_slots]
    )
    back = jnp.concatenate([back, jnp.zeros((1, part_rows, HD), back.dtype)], axis=0)
    outgoing_part = back[slot_entry]
    returned = lax.all_to_all(
        outgoing_part.reshape(pair_count, capacity, part_rows, HD),
        "ctx",
        split_axis=0,
        concat_axis=0,
        tiled=True,
    ).astype(jnp.float32)
    target = jnp.where(requested >= 0, requested, QB).reshape(-1)
    returned_sum = (
        jnp.zeros((QB + 1, part_rows, HD), jnp.float32)
        .at[target]
        .add(returned.reshape(-1, part_rows, HD))[:QB]
    )
    routed = lax.all_to_all(
        returned_sum.reshape(head_count, rows_here, part_rows, HD),
        "head",
        split_axis=0,
        concat_axis=0,
        tiled=True,
    )
    routed = jnp.transpose(routed, (1, 0, 2, 3)).reshape(rows_here, 2, BLK, HD)
    final = grad_tiles[:, 0] + routed
    return (
        outputs_rows[0],
        outputs_rows[1],
        final[:, 0].reshape(rows_here * BLK, HD).astype(jnp.bfloat16),
        final[:, 1].reshape(rows_here * BLK, HD).astype(jnp.bfloat16),
    )

def solution(mesh):
    return jax.shard_map(
        on_device,
        mesh=mesh,
        in_specs=(
            P("ctx", "head"),
            P("ctx", None),
            P("ctx", None),
            P("ctx", "head"),
            P("ctx", None),
        ),
        out_specs=(
            P("ctx", "head"),
            P("ctx", "head"),
            P(("ctx", "head"), None),
            P(("ctx", "head"), None),
        ),
        check_vma=False,
    )
```

```python
import math

import jax
import jax.numpy as jnp
from jax import lax
from jax.sharding import PartitionSpec as P

HD = 128
BLK = 128
SEL = 8
QB = 8


NEG_FILL = -1e30


def block_home(block, half_blocks, pair_count):
    stretch_idx = block // half_blocks
    early_side = stretch_idx < pair_count
    owner_dev = jnp.where(early_side, stretch_idx, 2 * pair_count - 1 - stretch_idx)
    local_blk = block % half_blocks + jnp.where(early_side, 0, half_blocks)
    return (owner_dev, local_blk)


def entry_slots(list_rows, half_blocks, pair_count):
    extras = list_rows[:, 1:].reshape(-1)
    usable = extras >= 0
    owner_dev, local_blk = block_home(jnp.maximum(extras, 0), half_blocks, pair_count)
    onehot_own = (
        (owner_dev[:, None] == jnp.arange(pair_count, dtype=jnp.int32)[None, :]) & usable[:, None]
    ).astype(jnp.int32)
    running = jnp.cumsum(onehot_own, axis=0)
    rank_in = jnp.sum(onehot_own * running, axis=1) - 1
    return (owner_dev, local_blk, rank_in, usable)


def head_exchange(x, head_idx, count):
    got = [lax.dynamic_index_in_dim(x, head_idx, axis=0, keepdims=False)]
    for k in range(1, count):
        piece = lax.dynamic_index_in_dim(x, (head_idx + k) % count, axis=0, keepdims=False)
        got.append(lax.ppermute(piece, "head", [(j, (j + k) % count) for j in range(count)]))
    order = (head_idx - jnp.arange(count, dtype=jnp.int32)) % count
    return jnp.stack(got)[order]


def rows_to_heads_split(x, head_count):
    rows, cols = x.shape
    parts = head_exchange(x.reshape(head_count, rows // head_count, cols), lax.axis_index("head"), head_count)
    return jnp.transpose(parts, (1, 0, 2)).reshape(rows // head_count, head_count * cols)


def heads_to_rows_split(y, head_count):
    rows, cols = y.shape
    parts = jnp.transpose(y.reshape(rows, head_count, cols // head_count), (1, 0, 2))
    parts = head_exchange(parts, lax.axis_index("head"), head_count)
    return parts.reshape(rows * head_count, cols // head_count)


def on_device(queries, key_rows, value_rows, out_grad, block_lists):
    pair_count = lax.axis_size("ctx")
    head_count = lax.axis_size("head")
    half_blocks = QB // 2
    capacity = (QB * (SEL - 1) + pair_count - 2) // (pair_count - 1)
    total_slots = pair_count * capacity
    device = lax.axis_index("ctx")
    head_idx = lax.axis_index("head")
    score_scale = 1.0 / math.sqrt(HD)
    rows_here = QB // head_count
    extras = SEL - 1
    entry_count = QB * extras
    my_entries = rows_here * extras
    part_rows = 2 * BLK // head_count
    owner_dev, local_blk, rank_in, usable = entry_slots(block_lists, half_blocks, pair_count)
    slot_idx = jnp.where(usable, owner_dev * capacity + rank_in, total_slots)
    req_table = (
        jnp.full((total_slots + 1,), -1, jnp.int32).at[slot_idx].set(local_blk)[:total_slots]
    )
    requested = lax.all_to_all(
        req_table.reshape(pair_count, capacity), "ctx", split_axis=0, concat_axis=0, tiled=True
    )
    q_rows = rows_to_heads_split(queries, head_count)
    g_rows = rows_to_heads_split(out_grad, head_count)
    heads_all = q_rows.shape[1] // HD
    kv_blocks = jnp.stack([key_rows.reshape(QB, BLK, HD), value_rows.reshape(QB, BLK, HD)], axis=1)
    kv_parts = kv_blocks.reshape(QB, head_count, part_rows, HD)
    my_part = lax.dynamic_index_in_dim(kv_parts, head_idx, axis=1, keepdims=False)
    send_parts = my_part[jnp.maximum(requested, 0)]
    fetched_part = lax.all_to_all(send_parts, "ctx", split_axis=0, concat_axis=0, tiled=True).reshape(
        total_slots, part_rows, HD
    )
    entry_slot = jnp.where(usable, slot_idx, 0).reshape(head_count, my_entries)
    share = fetched_part[entry_slot]
    got = lax.all_to_all(share, "head", split_axis=0, concat_axis=0, tiled=True)
    remote_kv = jnp.transpose(got, (1, 0, 2, 3)).reshape(rows_here, extras, 2, BLK, HD)
    first_row = head_idx * rows_here
    own_kv = lax.dynamic_slice_in_dim(kv_blocks, first_row, rows_here, axis=0)
    kv_tiles = jnp.concatenate([own_kv[:, None], remote_kv], axis=1)
    key_tile = kv_tiles[:, :, 0]
    value_tile = kv_tiles[:, :, 1]
    my_lists = lax.dynamic_slice_in_dim(block_lists, first_row, rows_here, axis=0)
    local_ids = first_row + jnp.arange(rows_here, dtype=jnp.int32)
    own_block = jnp.where(
        local_ids < half_blocks,
        device * half_blocks + local_ids,
        (2 * pair_count - 1 - device) * half_blocks + local_ids - half_blocks,
    )
    offsets = jnp.arange(BLK, dtype=jnp.int32)
    query_pos = own_block[:, None] * BLK + offsets[None, :]
    key_pos = jnp.maximum(my_lists, 0)[:, :, None] * BLK + offsets[None, None, :]
    visible = (my_lists >= 0)[:, None, :, None] & (
        key_pos[:, None, :, :] <= query_pos[:, :, None, None]
    )
    q_blocks = q_rows.reshape(rows_here, BLK, heads_all, HD)
    g_blocks = g_rows.reshape(rows_here, BLK, heads_all, HD)
    scores = (
        jnp.einsum("qihd,qsjd->qhisj", q_blocks, key_tile, preferred_element_type=jnp.float32)
        * score_scale
    )
    scores = jnp.where(visible[:, None], scores, NEG_FILL)
    row_max = jnp.max(scores, axis=(3, 4), keepdims=True)
    weights = jnp.exp(scores - row_max)
    row_total = jnp.sum(weights, axis=(3, 4), keepdims=True)
    summed = jnp.einsum(
        "qhisj,qsjd->qihd",
        weights.astype(jnp.bfloat16),
        value_tile,
        preferred_element_type=jnp.float32,
    )
    attended = (summed / jnp.transpose(row_total[..., 0, 0], (0, 2, 1))[..., None]).astype(
        jnp.bfloat16
    )
    log_total = row_max + jnp.log(row_total)
    probability = jnp.exp(scores - log_total)
    row_delta = jnp.sum(g_blocks.astype(jnp.float32) * attended.astype(jnp.float32), axis=3)
    grad_p = jnp.einsum(
        "qihd,qsjd->qhisj", g_blocks, value_tile, preferred_element_type=jnp.float32
    )
    grad_s = (probability * (grad_p - jnp.transpose(row_delta, (0, 2, 1))[..., None, None])).astype(
        jnp.bfloat16
    )
    query_grad = (
        jnp.einsum("qhisj,qsjd->qihd", grad_s, key_tile, preferred_element_type=jnp.float32)
        * score_scale
    ).astype(jnp.bfloat16)
    key_part = (
        jnp.einsum("qhisj,qihd->qsjd", grad_s, q_blocks, preferred_element_type=jnp.float32)
        * score_scale
    )
    value_part = jnp.einsum(
        "qhisj,qihd->qsjd",
        probability.astype(jnp.bfloat16),
        g_blocks,
        preferred_element_type=jnp.float32,
    )
    grad_tiles = jnp.stack([key_part, value_part], axis=2)
    remote_grad = grad_tiles[:, 1:].astype(jnp.bfloat16).reshape(my_entries, head_count, part_rows, HD)
    back = lax.all_to_all(
        jnp.transpose(remote_grad, (1, 0, 2, 3)), "head", split_axis=0, concat_axis=0, tiled=True
    ).reshape(entry_count, part_rows, HD)
    slot_entry = (
        jnp.full((total_slots + 1,), entry_count, jnp.int32)
        .at[slot_idx]
        .set(jnp.arange(entry_count, dtype=jnp.int32))[:total_slots]
    )
    back = jnp.concatenate([back, jnp.zeros((1, part_rows, HD), back.dtype)], axis=0)
    outgoing_part = back[slot_entry]
    returned = lax.all_to_all(
        outgoing_part.reshape(pair_count, capacity, part_rows, HD),
        "ctx",
        split_axis=0,
        concat_axis=0,
        tiled=True,
    ).astype(jnp.float32)
    target = jnp.where(requested >= 0, requested, QB).reshape(-1)
    returned_sum = (
        jnp.zeros((QB + 1, part_rows, HD), jnp.float32)
        .at[target]
        .add(returned.reshape(-1, part_rows, HD))[:QB]
    )
    routed = lax.all_to_all(
        returned_sum.reshape(head_count, rows_here, part_rows, HD),
        "head",
        split_axis=0,
        concat_axis=0,
        tiled=True,
    )
    routed = jnp.transpose(routed, (1, 0, 2, 3)).reshape(rows_here, 2, BLK, HD)
    final = grad_tiles[:, 0] + routed
    attended_out = heads_to_rows_split(attended.reshape(rows_here * BLK, heads_all * HD), head_count)
    query_grad_out = heads_to_rows_split(query_grad.reshape(rows_here * BLK, heads_all * HD), head_count)
    return (
        attended_out,
        query_grad_out,
        final[:, 0].reshape(rows_here * BLK, HD).astype(jnp.bfloat16),
        final[:, 1].reshape(rows_here * BLK, HD).astype(jnp.bfloat16),
    )

def solution(mesh):
    return jax.shard_map(
        on_device,
        mesh=mesh,
        in_specs=(
            P("ctx", "head"),
            P("ctx", None),
            P("ctx", None),
            P("ctx", "head"),
            P("ctx", None),
        ),
        out_specs=(
            P("ctx", "head"),
            P("ctx", "head"),
            P(("ctx", "head"), None),
            P(("ctx", "head"), None),
        ),
        check_vma=False,
    )
```

```python
import math

import jax
import jax.numpy as jnp
from jax import lax
from jax.sharding import PartitionSpec as P

HD = 128
BLK = 128
SEL = 8
QB = 8


NEG_FILL = -1e30


def block_home(block, half_blocks, pair_count):
    stretch_idx = block // half_blocks
    early_side = stretch_idx < pair_count
    owner_dev = jnp.where(early_side, stretch_idx, 2 * pair_count - 1 - stretch_idx)
    local_blk = block % half_blocks + jnp.where(early_side, 0, half_blocks)
    return (owner_dev, local_blk)


def entry_slots(list_rows, half_blocks, pair_count):
    extras = list_rows[:, 1:].reshape(-1)
    usable = extras >= 0
    owner_dev, local_blk = block_home(jnp.maximum(extras, 0), half_blocks, pair_count)
    onehot_own = (
        (owner_dev[:, None] == jnp.arange(pair_count, dtype=jnp.int32)[None, :]) & usable[:, None]
    ).astype(jnp.int32)
    running = jnp.cumsum(onehot_own, axis=0)
    rank_in = jnp.sum(onehot_own * running, axis=1) - 1
    return (owner_dev, local_blk, rank_in, usable)


def head_exchange(x, head_idx, count):
    got = [lax.dynamic_index_in_dim(x, head_idx, axis=0, keepdims=False)]
    for k in range(1, count):
        piece = lax.dynamic_index_in_dim(x, (head_idx + k) % count, axis=0, keepdims=False)
        got.append(lax.ppermute(piece, "head", [(j, (j + k) % count) for j in range(count)]))
    order = (head_idx - jnp.arange(count, dtype=jnp.int32)) % count
    return jnp.stack(got)[order]


def rows_to_heads_split(x, head_count):
    rows, cols = x.shape
    parts = head_exchange(x.reshape(head_count, rows // head_count, cols), lax.axis_index("head"), head_count)
    return jnp.transpose(parts, (1, 0, 2)).reshape(rows // head_count, head_count * cols)


def heads_to_rows_split(y, head_count):
    rows, cols = y.shape
    parts = jnp.transpose(y.reshape(rows, head_count, cols // head_count), (1, 0, 2))
    parts = head_exchange(parts, lax.axis_index("head"), head_count)
    return parts.reshape(rows * head_count, cols // head_count)


def on_device(queries, key_rows, value_rows, out_grad, block_lists):
    pair_count = lax.axis_size("ctx")
    head_count = lax.axis_size("head")
    half_blocks = QB // 2
    capacity = (QB * (SEL - 1) + pair_count - 2) // (pair_count - 1)
    total_slots = pair_count * capacity
    device = lax.axis_index("ctx")
    head_idx = lax.axis_index("head")
    score_scale = 1.0 / math.sqrt(HD)
    rows_here = QB // head_count
    extras = SEL - 1
    entry_count = QB * extras
    my_entries = rows_here * extras
    part_rows = 2 * BLK // head_count
    owner_dev, local_blk, rank_in, usable = entry_slots(block_lists, half_blocks, pair_count)
    slot_idx = jnp.where(usable, owner_dev * capacity + rank_in, total_slots)
    req_table = (
        jnp.full((total_slots + 1,), -1, jnp.int32).at[slot_idx].set(local_blk)[:total_slots]
    )
    requested = lax.all_to_all(
        req_table.reshape(pair_count, capacity), "ctx", split_axis=0, concat_axis=0, tiled=True
    )
    q_rows = rows_to_heads_split(queries, head_count)
    g_rows = rows_to_heads_split(out_grad, head_count)
    heads_all = q_rows.shape[1] // HD
    kv_blocks = jnp.stack([key_rows.reshape(QB, BLK, HD), value_rows.reshape(QB, BLK, HD)], axis=1)
    kv_parts = kv_blocks.reshape(QB, head_count, part_rows, HD)
    my_part = lax.dynamic_index_in_dim(kv_parts, head_idx, axis=1, keepdims=False)
    send_parts = my_part[jnp.maximum(requested, 0)]
    fetched_part = lax.all_to_all(send_parts, "ctx", split_axis=0, concat_axis=0, tiled=True).reshape(
        total_slots, part_rows, HD
    )
    entry_slot = jnp.where(usable, slot_idx, 0).reshape(head_count, my_entries)
    share = fetched_part[entry_slot]
    got = head_exchange(share, head_idx, head_count)
    remote_kv = jnp.transpose(got, (1, 0, 2, 3)).reshape(rows_here, extras, 2, BLK, HD)
    first_row = head_idx * rows_here
    own_kv = lax.dynamic_slice_in_dim(kv_blocks, first_row, rows_here, axis=0)
    kv_tiles = jnp.concatenate([own_kv[:, None], remote_kv], axis=1)
    key_tile = kv_tiles[:, :, 0]
    value_tile = kv_tiles[:, :, 1]
    my_lists = lax.dynamic_slice_in_dim(block_lists, first_row, rows_here, axis=0)
    local_ids = first_row + jnp.arange(rows_here, dtype=jnp.int32)
    own_block = jnp.where(
        local_ids < half_blocks,
        device * half_blocks + local_ids,
        (2 * pair_count - 1 - device) * half_blocks + local_ids - half_blocks,
    )
    offsets = jnp.arange(BLK, dtype=jnp.int32)
    query_pos = own_block[:, None] * BLK + offsets[None, :]
    key_pos = jnp.maximum(my_lists, 0)[:, :, None] * BLK + offsets[None, None, :]
    visible = (my_lists >= 0)[:, None, :, None] & (
        key_pos[:, None, :, :] <= query_pos[:, :, None, None]
    )
    q_blocks = q_rows.reshape(rows_here, BLK, heads_all, HD)
    g_blocks = g_rows.reshape(rows_here, BLK, heads_all, HD)
    scores = (
        jnp.einsum("qihd,qsjd->qhisj", q_blocks, key_tile, preferred_element_type=jnp.float32)
        * score_scale
    )
    scores = jnp.where(visible[:, None], scores, NEG_FILL)
    row_max = jnp.max(scores, axis=(3, 4), keepdims=True)
    weights = jnp.exp(scores - row_max)
    row_total = jnp.sum(weights, axis=(3, 4), keepdims=True)
    summed = jnp.einsum(
        "qhisj,qsjd->qihd",
        weights.astype(jnp.bfloat16),
        value_tile,
        preferred_element_type=jnp.float32,
    )
    attended = (summed / jnp.transpose(row_total[..., 0, 0], (0, 2, 1))[..., None]).astype(
        jnp.bfloat16
    )
    log_total = row_max + jnp.log(row_total)
    probability = jnp.exp(scores - log_total)
    row_delta = jnp.sum(g_blocks.astype(jnp.float32) * attended.astype(jnp.float32), axis=3)
    grad_p = jnp.einsum(
        "qihd,qsjd->qhisj", g_blocks, value_tile, preferred_element_type=jnp.float32
    )
    grad_s = (probability * (grad_p - jnp.transpose(row_delta, (0, 2, 1))[..., None, None])).astype(
        jnp.bfloat16
    )
    query_grad = (
        jnp.einsum("qhisj,qsjd->qihd", grad_s, key_tile, preferred_element_type=jnp.float32)
        * score_scale
    ).astype(jnp.bfloat16)
    key_part = (
        jnp.einsum("qhisj,qihd->qsjd", grad_s, q_blocks, preferred_element_type=jnp.float32)
        * score_scale
    )
    value_part = jnp.einsum(
        "qhisj,qihd->qsjd",
        probability.astype(jnp.bfloat16),
        g_blocks,
        preferred_element_type=jnp.float32,
    )
    grad_tiles = jnp.stack([key_part, value_part], axis=2)
    remote_grad = grad_tiles[:, 1:].astype(jnp.bfloat16).reshape(my_entries, head_count, part_rows, HD)
    back = head_exchange(jnp.transpose(remote_grad, (1, 0, 2, 3)), head_idx, head_count).reshape(
        entry_count, part_rows, HD
    )
    slot_entry = (
        jnp.full((total_slots + 1,), entry_count, jnp.int32)
        .at[slot_idx]
        .set(jnp.arange(entry_count, dtype=jnp.int32))[:total_slots]
    )
    back = jnp.concatenate([back, jnp.zeros((1, part_rows, HD), back.dtype)], axis=0)
    outgoing_part = back[slot_entry]
    returned = lax.all_to_all(
        outgoing_part.reshape(pair_count, capacity, part_rows, HD),
        "ctx",
        split_axis=0,
        concat_axis=0,
        tiled=True,
    ).astype(jnp.float32)
    target = jnp.where(requested >= 0, requested, QB).reshape(-1)
    returned_sum = (
        jnp.zeros((QB + 1, part_rows, HD), jnp.float32)
        .at[target]
        .add(returned.reshape(-1, part_rows, HD))[:QB]
    )
    routed = head_exchange(returned_sum.reshape(head_count, rows_here, part_rows, HD), head_idx, head_count)
    routed = jnp.transpose(routed, (1, 0, 2, 3)).reshape(rows_here, 2, BLK, HD)
    final = grad_tiles[:, 0] + routed
    attended_out = heads_to_rows_split(attended.reshape(rows_here * BLK, heads_all * HD), head_count)
    query_grad_out = heads_to_rows_split(query_grad.reshape(rows_here * BLK, heads_all * HD), head_count)
    return (
        attended_out,
        query_grad_out,
        final[:, 0].reshape(rows_here * BLK, HD).astype(jnp.bfloat16),
        final[:, 1].reshape(rows_here * BLK, HD).astype(jnp.bfloat16),
    )

def solution(mesh):
    return jax.shard_map(
        on_device,
        mesh=mesh,
        in_specs=(
            P("ctx", "head"),
            P("ctx", None),
            P("ctx", None),
            P("ctx", "head"),
            P("ctx", None),
        ),
        out_specs=(
            P("ctx", "head"),
            P("ctx", "head"),
            P(("ctx", "head"), None),
            P(("ctx", "head"), None),
        ),
        check_vma=False,
    )
```

```python
import math

import jax
import jax.numpy as jnp
from jax import lax
from jax.sharding import PartitionSpec as P

HD = 128
BLK = 128
SEL = 8
QB = 8


NEG_FILL = -1e30


def block_home(block, half_blocks, pair_count):
    stretch_idx = block // half_blocks
    early_side = stretch_idx < pair_count
    owner_dev = jnp.where(early_side, stretch_idx, 2 * pair_count - 1 - stretch_idx)
    local_blk = block % half_blocks + jnp.where(early_side, 0, half_blocks)
    return (owner_dev, local_blk)


def entry_slots(list_rows, half_blocks, pair_count):
    extras = list_rows[:, 1:].reshape(-1)
    usable = extras >= 0
    owner_dev, local_blk = block_home(jnp.maximum(extras, 0), half_blocks, pair_count)
    onehot_own = (
        (owner_dev[:, None] == jnp.arange(pair_count, dtype=jnp.int32)[None, :]) & usable[:, None]
    ).astype(jnp.int32)
    running = jnp.cumsum(onehot_own, axis=0)
    rank_in = jnp.sum(onehot_own * running, axis=1) - 1
    return (owner_dev, local_blk, rank_in, usable)


def head_exchange(x, head_idx, count):
    ahead = x[(head_idx + jnp.arange(count, dtype=jnp.int32)) % count]
    got = [ahead[0]]
    for k in range(1, count):
        got.append(lax.ppermute(ahead[k], "head", [(j, (j + k) % count) for j in range(count)]))
    order = (head_idx - jnp.arange(count, dtype=jnp.int32)) % count
    return jnp.stack(got)[order]


def on_device(queries, key_rows, value_rows, out_grad, block_lists):
    pair_count = lax.axis_size("ctx")
    head_count = lax.axis_size("head")
    half_blocks = QB // 2
    capacity = (QB * (SEL - 1) + pair_count - 2) // (pair_count - 1)
    total_slots = pair_count * capacity
    device = lax.axis_index("ctx")
    head_idx = lax.axis_index("head")
    score_scale = 1.0 / math.sqrt(HD)
    rows_here = QB // head_count
    extras = SEL - 1
    entry_count = QB * extras
    my_entries = rows_here * extras
    part_rows = 2 * BLK // head_count
    owner_dev, local_blk, rank_in, usable = entry_slots(block_lists, half_blocks, pair_count)
    slot_idx = jnp.where(usable, owner_dev * capacity + rank_in, total_slots)
    req_table = (
        jnp.full((total_slots + 1,), -1, jnp.int32).at[slot_idx].set(local_blk)[:total_slots]
    )
    requested = lax.all_to_all(
        req_table.reshape(pair_count, capacity), "ctx", split_axis=0, concat_axis=0, tiled=True
    )
    rows_in, cols_in = queries.shape
    inputs_split = jnp.stack(
        [
            queries.reshape(head_count, rows_in // head_count, cols_in),
            out_grad.reshape(head_count, rows_in // head_count, cols_in),
        ],
        axis=1,
    )
    inputs_rows = head_exchange(inputs_split, head_idx, head_count)
    inputs_rows = jnp.transpose(inputs_rows, (1, 2, 0, 3)).reshape(2, rows_in // head_count, head_count * cols_in)
    q_rows = inputs_rows[0]
    g_rows = inputs_rows[1]
    heads_all = q_rows.shape[1] // HD
    kv_blocks = jnp.stack([key_rows.reshape(QB, BLK, HD), value_rows.reshape(QB, BLK, HD)], axis=1)
    kv_parts = kv_blocks.reshape(QB, head_count, part_rows, HD)
    my_part = lax.dynamic_index_in_dim(kv_parts, head_idx, axis=1, keepdims=False)
    send_parts = my_part[jnp.maximum(requested, 0)]
    fetched_part = lax.all_to_all(send_parts, "ctx", split_axis=0, concat_axis=0, tiled=True).reshape(
        total_slots, part_rows, HD
    )
    entry_slot = jnp.where(usable, slot_idx, 0).reshape(head_count, my_entries)
    share = fetched_part[entry_slot]
    got = head_exchange(share, head_idx, head_count)
    remote_kv = jnp.transpose(got, (1, 0, 2, 3)).reshape(rows_here, extras, 2, BLK, HD)
    first_row = head_idx * rows_here
    own_kv = lax.dynamic_slice_in_dim(kv_blocks, first_row, rows_here, axis=0)
    kv_tiles = jnp.concatenate([own_kv[:, None], remote_kv], axis=1)
    key_tile = kv_tiles[:, :, 0]
    value_tile = kv_tiles[:, :, 1]
    my_lists = lax.dynamic_slice_in_dim(block_lists, first_row, rows_here, axis=0)
    local_ids = first_row + jnp.arange(rows_here, dtype=jnp.int32)
    own_block = jnp.where(
        local_ids < half_blocks,
        device * half_blocks + local_ids,
        (2 * pair_count - 1 - device) * half_blocks + local_ids - half_blocks,
    )
    offsets = jnp.arange(BLK, dtype=jnp.int32)
    query_pos = own_block[:, None] * BLK + offsets[None, :]
    key_pos = jnp.maximum(my_lists, 0)[:, :, None] * BLK + offsets[None, None, :]
    visible = (my_lists >= 0)[:, None, :, None] & (
        key_pos[:, None, :, :] <= query_pos[:, :, None, None]
    )
    q_blocks = q_rows.reshape(rows_here, BLK, heads_all, HD)
    g_blocks = g_rows.reshape(rows_here, BLK, heads_all, HD)
    scores = (
        jnp.einsum("qihd,qsjd->qhisj", q_blocks, key_tile, preferred_element_type=jnp.float32)
        * score_scale
    )
    scores = jnp.where(visible[:, None], scores, NEG_FILL)
    row_max = jnp.max(scores, axis=(3, 4), keepdims=True)
    weights = jnp.exp(scores - row_max)
    row_total = jnp.sum(weights, axis=(3, 4), keepdims=True)
    summed = jnp.einsum(
        "qhisj,qsjd->qihd",
        weights.astype(jnp.bfloat16),
        value_tile,
        preferred_element_type=jnp.float32,
    )
    attended = (summed / jnp.transpose(row_total[..., 0, 0], (0, 2, 1))[..., None]).astype(
        jnp.bfloat16
    )
    log_total = row_max + jnp.log(row_total)
    probability = jnp.exp(scores - log_total)
    row_delta = jnp.sum(g_blocks.astype(jnp.float32) * attended.astype(jnp.float32), axis=3)
    grad_p = jnp.einsum(
        "qihd,qsjd->qhisj", g_blocks, value_tile, preferred_element_type=jnp.float32
    )
    grad_s = (probability * (grad_p - jnp.transpose(row_delta, (0, 2, 1))[..., None, None])).astype(
        jnp.bfloat16
    )
    query_grad = (
        jnp.einsum("qhisj,qsjd->qihd", grad_s, key_tile, preferred_element_type=jnp.float32)
        * score_scale
    ).astype(jnp.bfloat16)
    key_part = (
        jnp.einsum("qhisj,qihd->qsjd", grad_s, q_blocks, preferred_element_type=jnp.float32)
        * score_scale
    )
    value_part = jnp.einsum(
        "qhisj,qihd->qsjd",
        probability.astype(jnp.bfloat16),
        g_blocks,
        preferred_element_type=jnp.float32,
    )
    grad_tiles = jnp.stack([key_part, value_part], axis=2)
    remote_grad = grad_tiles[:, 1:].astype(jnp.bfloat16).reshape(my_entries, head_count, part_rows, HD)
    back = head_exchange(jnp.transpose(remote_grad, (1, 0, 2, 3)), head_idx, head_count).reshape(
        entry_count, part_rows, HD
    )
    slot_entry = (
        jnp.full((total_slots + 1,), entry_count, jnp.int32)
        .at[slot_idx]
        .set(jnp.arange(entry_count, dtype=jnp.int32))[:total_slots]
    )
    back = jnp.concatenate([back, jnp.zeros((1, part_rows, HD), back.dtype)], axis=0)
    outgoing_part = back[slot_entry]
    returned = lax.all_to_all(
        outgoing_part.reshape(pair_count, capacity, part_rows, HD),
        "ctx",
        split_axis=0,
        concat_axis=0,
        tiled=True,
    ).astype(jnp.float32)
    target = jnp.where(requested >= 0, requested, QB).reshape(-1)
    returned_sum = (
        jnp.zeros((QB + 1, part_rows, HD), jnp.float32)
        .at[target]
        .add(returned.reshape(-1, part_rows, HD))[:QB]
    )
    routed = head_exchange(returned_sum.reshape(head_count, rows_here, part_rows, HD), head_idx, head_count)
    routed = jnp.transpose(routed, (1, 0, 2, 3)).reshape(rows_here, 2, BLK, HD)
    final = grad_tiles[:, 0] + routed
    out_rows = rows_here * BLK
    out_cols = heads_all * HD // head_count
    outputs_split = jnp.transpose(
        jnp.stack([attended, query_grad]).reshape(2, out_rows, head_count, out_cols), (2, 0, 1, 3)
    )
    outputs_rows = head_exchange(outputs_split, head_idx, head_count)
    return (
        outputs_rows[:, 0].reshape(head_count * out_rows, out_cols),
        outputs_rows[:, 1].reshape(head_count * out_rows, out_cols),
        final[:, 0].reshape(rows_here * BLK, HD).astype(jnp.bfloat16),
        final[:, 1].reshape(rows_here * BLK, HD).astype(jnp.bfloat16),
    )

def solution(mesh):
    return jax.shard_map(
        on_device,
        mesh=mesh,
        in_specs=(
            P("ctx", "head"),
            P("ctx", None),
            P("ctx", None),
            P("ctx", "head"),
            P("ctx", None),
        ),
        out_specs=(
            P("ctx", "head"),
            P("ctx", "head"),
            P(("ctx", "head"), None),
            P(("ctx", "head"), None),
        ),
        check_vma=False,
    )
```

```python
import math

import jax
import jax.numpy as jnp
from jax import lax
from jax.sharding import PartitionSpec as P

HD = 128
BLK = 128
SEL = 8
QB = 8


NEG_FILL = -1e30


def block_home(block, half_blocks, pair_count):
    stretch_idx = block // half_blocks
    early_side = stretch_idx < pair_count
    owner_dev = jnp.where(early_side, stretch_idx, 2 * pair_count - 1 - stretch_idx)
    local_blk = block % half_blocks + jnp.where(early_side, 0, half_blocks)
    return (owner_dev, local_blk)


def entry_slots(list_rows, half_blocks, pair_count):
    extras = list_rows[:, 1:].reshape(-1)
    usable = extras >= 0
    owner_dev, local_blk = block_home(jnp.maximum(extras, 0), half_blocks, pair_count)
    onehot_own = (
        (owner_dev[:, None] == jnp.arange(pair_count, dtype=jnp.int32)[None, :]) & usable[:, None]
    ).astype(jnp.int32)
    running = jnp.cumsum(onehot_own, axis=0)
    rank_in = jnp.sum(onehot_own * running, axis=1) - 1
    return (owner_dev, local_blk, rank_in, usable)


def head_exchange(x, head_idx, count):
    ahead = x[(head_idx + jnp.arange(count, dtype=jnp.int32)) % count]
    got = [ahead[0]]
    for k in range(1, count):
        got.append(lax.ppermute(ahead[k], "head", [(j, (j + k) % count) for j in range(count)]))
    order = (head_idx - jnp.arange(count, dtype=jnp.int32)) % count
    return jnp.stack(got)[order]


def on_device(queries, key_rows, value_rows, out_grad, block_lists):
    pair_count = lax.axis_size("ctx")
    head_count = lax.axis_size("head")
    half_blocks = QB // 2
    capacity = (QB * (SEL - 1) + pair_count - 2) // (pair_count - 1)
    total_slots = pair_count * capacity
    device = lax.axis_index("ctx")
    head_idx = lax.axis_index("head")
    score_scale = 1.0 / math.sqrt(HD)
    rows_here = QB // head_count
    extras = SEL - 1
    entry_count = QB * extras
    my_entries = rows_here * extras
    part_rows = 2 * BLK // head_count
    owner_dev, local_blk, rank_in, usable = entry_slots(block_lists, half_blocks, pair_count)
    slot_idx = jnp.where(usable, owner_dev * capacity + rank_in, total_slots)
    req_table = (
        jnp.full((total_slots + 1,), -1, jnp.int32).at[slot_idx].set(local_blk)[:total_slots]
    )
    all_lists = lax.all_gather(block_lists, "ctx", axis=0, tiled=True)
    all_extras = all_lists[:, 1:].reshape(pair_count, entry_count)
    all_owner, all_local = block_home(jnp.maximum(all_extras, 0), half_blocks, pair_count)
    asks_me = (all_extras >= 0) & (all_owner == device)
    ask_rank = jnp.cumsum(asks_me.astype(jnp.int32), axis=1) - 1
    hit = asks_me[:, :, None] & (ask_rank[:, :, None] == jnp.arange(capacity, dtype=jnp.int32)[None, None, :])
    requested = jnp.sum(jnp.where(hit, all_local[:, :, None] + 1, 0), axis=1) - 1
    rows_in, cols_in = queries.shape
    inputs_split = jnp.stack(
        [
            queries.reshape(head_count, rows_in // head_count, cols_in),
            out_grad.reshape(head_count, rows_in // head_count, cols_in),
        ],
        axis=1,
    )
    inputs_rows = head_exchange(inputs_split, head_idx, head_count)
    inputs_rows = jnp.transpose(inputs_rows, (1, 2, 0, 3)).reshape(2, rows_in // head_count, head_count * cols_in)
    q_rows = inputs_rows[0]
    g_rows = inputs_rows[1]
    heads_all = q_rows.shape[1] // HD
    kv_blocks = jnp.stack([key_rows.reshape(QB, BLK, HD), value_rows.reshape(QB, BLK, HD)], axis=1)
    kv_parts = kv_blocks.reshape(QB, head_count, part_rows, HD)
    my_part = lax.dynamic_index_in_dim(kv_parts, head_idx, axis=1, keepdims=False)
    send_parts = my_part[jnp.maximum(requested, 0)]
    fetched_part = lax.all_to_all(send_parts, "ctx", split_axis=0, concat_axis=0, tiled=True).reshape(
        total_slots, part_rows, HD
    )
    entry_slot = jnp.where(usable, slot_idx, 0).reshape(head_count, my_entries)
    share = fetched_part[entry_slot]
    got = head_exchange(share, head_idx, head_count)
    remote_kv = jnp.transpose(got, (1, 0, 2, 3)).reshape(rows_here, extras, 2, BLK, HD)
    first_row = head_idx * rows_here
    own_kv = lax.dynamic_slice_in_dim(kv_blocks, first_row, rows_here, axis=0)
    kv_tiles = jnp.concatenate([own_kv[:, None], remote_kv], axis=1)
    key_tile = kv_tiles[:, :, 0]
    value_tile = kv_tiles[:, :, 1]
    my_lists = lax.dynamic_slice_in_dim(block_lists, first_row, rows_here, axis=0)
    local_ids = first_row + jnp.arange(rows_here, dtype=jnp.int32)
    own_block = jnp.where(
        local_ids < half_blocks,
        device * half_blocks + local_ids,
        (2 * pair_count - 1 - device) * half_blocks + local_ids - half_blocks,
    )
    offsets = jnp.arange(BLK, dtype=jnp.int32)
    query_pos = own_block[:, None] * BLK + offsets[None, :]
    key_pos = jnp.maximum(my_lists, 0)[:, :, None] * BLK + offsets[None, None, :]
    visible = (my_lists >= 0)[:, None, :, None] & (
        key_pos[:, None, :, :] <= query_pos[:, :, None, None]
    )
    q_blocks = q_rows.reshape(rows_here, BLK, heads_all, HD)
    g_blocks = g_rows.reshape(rows_here, BLK, heads_all, HD)
    scores = (
        jnp.einsum("qihd,qsjd->qhisj", q_blocks, key_tile, preferred_element_type=jnp.float32)
        * score_scale
    )
    scores = jnp.where(visible[:, None], scores, NEG_FILL)
    row_max = jnp.max(scores, axis=(3, 4), keepdims=True)
    weights = jnp.exp(scores - row_max)
    row_total = jnp.sum(weights, axis=(3, 4), keepdims=True)
    summed = jnp.einsum(
        "qhisj,qsjd->qihd",
        weights.astype(jnp.bfloat16),
        value_tile,
        preferred_element_type=jnp.float32,
    )
    attended = (summed / jnp.transpose(row_total[..., 0, 0], (0, 2, 1))[..., None]).astype(
        jnp.bfloat16
    )
    log_total = row_max + jnp.log(row_total)
    probability = jnp.exp(scores - log_total)
    row_delta = jnp.sum(g_blocks.astype(jnp.float32) * attended.astype(jnp.float32), axis=3)
    grad_p = jnp.einsum(
        "qihd,qsjd->qhisj", g_blocks, value_tile, preferred_element_type=jnp.float32
    )
    grad_s = (probability * (grad_p - jnp.transpose(row_delta, (0, 2, 1))[..., None, None])).astype(
        jnp.bfloat16
    )
    query_grad = (
        jnp.einsum("qhisj,qsjd->qihd", grad_s, key_tile, preferred_element_type=jnp.float32)
        * score_scale
    ).astype(jnp.bfloat16)
    key_part = (
        jnp.einsum("qhisj,qihd->qsjd", grad_s, q_blocks, preferred_element_type=jnp.float32)
        * score_scale
    )
    value_part = jnp.einsum(
        "qhisj,qihd->qsjd",
        probability.astype(jnp.bfloat16),
        g_blocks,
        preferred_element_type=jnp.float32,
    )
    grad_tiles = jnp.stack([key_part, value_part], axis=2)
    remote_grad = grad_tiles[:, 1:].astype(jnp.bfloat16).reshape(my_entries, head_count, part_rows, HD)
    back = head_exchange(jnp.transpose(remote_grad, (1, 0, 2, 3)), head_idx, head_count).reshape(
        entry_count, part_rows, HD
    )
    slot_entry = (
        jnp.full((total_slots + 1,), entry_count, jnp.int32)
        .at[slot_idx]
        .set(jnp.arange(entry_count, dtype=jnp.int32))[:total_slots]
    )
    back = jnp.concatenate([back, jnp.zeros((1, part_rows, HD), back.dtype)], axis=0)
    outgoing_part = back[slot_entry]
    returned = lax.all_to_all(
        outgoing_part.reshape(pair_count, capacity, part_rows, HD),
        "ctx",
        split_axis=0,
        concat_axis=0,
        tiled=True,
    ).astype(jnp.float32)
    target = jnp.where(requested >= 0, requested, QB).reshape(-1)
    returned_sum = (
        jnp.zeros((QB + 1, part_rows, HD), jnp.float32)
        .at[target]
        .add(returned.reshape(-1, part_rows, HD))[:QB]
    )
    routed = head_exchange(returned_sum.reshape(head_count, rows_here, part_rows, HD), head_idx, head_count)
    routed = jnp.transpose(routed, (1, 0, 2, 3)).reshape(rows_here, 2, BLK, HD)
    final = grad_tiles[:, 0] + routed
    out_rows = rows_here * BLK
    out_cols = heads_all * HD // head_count
    outputs_split = jnp.transpose(
        jnp.stack([attended, query_grad]).reshape(2, out_rows, head_count, out_cols), (2, 0, 1, 3)
    )
    outputs_rows = head_exchange(outputs_split, head_idx, head_count)
    return (
        outputs_rows[:, 0].reshape(head_count * out_rows, out_cols),
        outputs_rows[:, 1].reshape(head_count * out_rows, out_cols),
        final[:, 0].reshape(rows_here * BLK, HD).astype(jnp.bfloat16),
        final[:, 1].reshape(rows_here * BLK, HD).astype(jnp.bfloat16),
    )

def solution(mesh):
    return jax.shard_map(
        on_device,
        mesh=mesh,
        in_specs=(
            P("ctx", "head"),
            P("ctx", None),
            P("ctx", None),
            P("ctx", "head"),
            P("ctx", None),
        ),
        out_specs=(
            P("ctx", "head"),
            P("ctx", "head"),
            P(("ctx", "head"), None),
            P(("ctx", "head"), None),
        ),
        check_vma=False,
    )
```

```python
import math

import jax
import jax.numpy as jnp
from jax import lax
from jax.sharding import PartitionSpec as P

HD = 128
BLK = 128
SEL = 8
QB = 8


NEG_FILL = -1e30


def block_home(block, half_blocks, pair_count):
    stretch_idx = block // half_blocks
    early_side = stretch_idx < pair_count
    owner_dev = jnp.where(early_side, stretch_idx, 2 * pair_count - 1 - stretch_idx)
    local_blk = block % half_blocks + jnp.where(early_side, 0, half_blocks)
    return (owner_dev, local_blk)


def entry_slots(list_rows, half_blocks, pair_count):
    extras = list_rows[:, 1:].reshape(-1)
    usable = extras >= 0
    owner_dev, local_blk = block_home(jnp.maximum(extras, 0), half_blocks, pair_count)
    onehot_own = (
        (owner_dev[:, None] == jnp.arange(pair_count, dtype=jnp.int32)[None, :]) & usable[:, None]
    ).astype(jnp.int32)
    running = jnp.cumsum(onehot_own, axis=0)
    rank_in = jnp.sum(onehot_own * running, axis=1) - 1
    return (owner_dev, local_blk, rank_in, usable)


def head_exchange(x, head_idx, count):
    ahead = x[(head_idx + jnp.arange(count, dtype=jnp.int32)) % count]
    got = [ahead[0]]
    for k in range(1, count):
        got.append(lax.ppermute(ahead[k], "head", [(j, (j + k) % count) for j in range(count)]))
    order = (head_idx - jnp.arange(count, dtype=jnp.int32)) % count
    return jnp.stack(got)[order]


def on_device(queries, key_rows, value_rows, out_grad, block_lists):
    pair_count = lax.axis_size("ctx")
    head_count = lax.axis_size("head")
    half_blocks = QB // 2
    capacity = (QB * (SEL - 1) + pair_count - 2) // (pair_count - 1)
    total_slots = pair_count * capacity
    device = lax.axis_index("ctx")
    head_idx = lax.axis_index("head")
    score_scale = 1.0 / math.sqrt(HD)
    rows_here = QB // head_count
    extras = SEL - 1
    entry_count = QB * extras
    my_entries = rows_here * extras
    part_rows = 2 * BLK // head_count
    owner_dev, local_blk, rank_in, usable = entry_slots(block_lists, half_blocks, pair_count)
    slot_idx = jnp.where(usable, owner_dev * capacity + rank_in, total_slots)
    req_table = (
        jnp.full((total_slots + 1,), -1, jnp.int32).at[slot_idx].set(local_blk)[:total_slots]
    )
    requested = lax.all_to_all(
        req_table.reshape(pair_count, capacity), "ctx", split_axis=0, concat_axis=0, tiled=True
    )
    rows_in, cols_in = queries.shape
    inputs_split = jnp.stack(
        [
            queries.reshape(head_count, rows_in // head_count, cols_in),
            out_grad.reshape(head_count, rows_in // head_count, cols_in),
        ],
        axis=1,
    )
    inputs_rows = head_exchange(inputs_split, head_idx, head_count)
    inputs_rows = jnp.transpose(inputs_rows, (1, 2, 0, 3)).reshape(2, rows_in // head_count, head_count * cols_in)
    q_rows = inputs_rows[0]
    g_rows = inputs_rows[1]
    heads_all = q_rows.shape[1] // HD
    kv_blocks = jnp.stack([key_rows.reshape(QB, BLK, HD), value_rows.reshape(QB, BLK, HD)], axis=1)
    kv_parts = kv_blocks.reshape(QB, head_count, part_rows, HD)
    my_part = lax.dynamic_index_in_dim(kv_parts, head_idx, axis=1, keepdims=False)
    send_parts = my_part[jnp.maximum(requested, 0)]
    fetched_part = lax.all_to_all(send_parts, "ctx", split_axis=0, concat_axis=0, tiled=True).reshape(
        total_slots, part_rows, HD
    )
    entry_slot = jnp.where(usable, slot_idx, 0).reshape(head_count, my_entries)
    share = fetched_part[entry_slot]
    got = head_exchange(share, head_idx, head_count)
    remote_kv = jnp.transpose(got, (1, 0, 2, 3)).reshape(rows_here, extras, 2, BLK, HD)
    first_row = head_idx * rows_here
    own_kv = lax.dynamic_slice_in_dim(kv_blocks, first_row, rows_here, axis=0)
    kv_tiles = jnp.concatenate([own_kv[:, None], remote_kv], axis=1)
    key_tile = kv_tiles[:, :, 0]
    value_tile = kv_tiles[:, :, 1]
    my_lists = lax.dynamic_slice_in_dim(block_lists, first_row, rows_here, axis=0)
    local_ids = first_row + jnp.arange(rows_here, dtype=jnp.int32)
    own_block = jnp.where(
        local_ids < half_blocks,
        device * half_blocks + local_ids,
        (2 * pair_count - 1 - device) * half_blocks + local_ids - half_blocks,
    )
    offsets = jnp.arange(BLK, dtype=jnp.int32)
    query_pos = own_block[:, None] * BLK + offsets[None, :]
    key_pos = jnp.maximum(my_lists, 0)[:, :, None] * BLK + offsets[None, None, :]
    visible = (my_lists >= 0)[:, None, :, None] & (
        key_pos[:, None, :, :] <= query_pos[:, :, None, None]
    )
    q_blocks = q_rows.reshape(rows_here, BLK, heads_all, HD)
    g_blocks = g_rows.reshape(rows_here, BLK, heads_all, HD)
    scores = (
        jnp.einsum("qihd,qsjd->qhisj", q_blocks, key_tile, preferred_element_type=jnp.float32)
        * score_scale
    )
    scores = jnp.where(visible[:, None], scores, NEG_FILL)
    row_max = jnp.max(scores, axis=(3, 4), keepdims=True)
    weights = jnp.exp(scores - row_max)
    row_total = jnp.sum(weights, axis=(3, 4), keepdims=True)
    summed = jnp.einsum(
        "qhisj,qsjd->qihd",
        weights.astype(jnp.bfloat16),
        value_tile,
        preferred_element_type=jnp.float32,
    )
    attended = (summed / jnp.transpose(row_total[..., 0, 0], (0, 2, 1))[..., None]).astype(
        jnp.bfloat16
    )
    log_total = row_max + jnp.log(row_total)
    probability = jnp.exp(scores - log_total)
    row_delta = jnp.sum(g_blocks.astype(jnp.float32) * attended.astype(jnp.float32), axis=3)
    grad_p = jnp.einsum(
        "qihd,qsjd->qhisj", g_blocks, value_tile, preferred_element_type=jnp.float32
    )
    grad_s = (probability * (grad_p - jnp.transpose(row_delta, (0, 2, 1))[..., None, None])).astype(
        jnp.bfloat16
    )
    query_grad = (
        jnp.einsum("qhisj,qsjd->qihd", grad_s, key_tile, preferred_element_type=jnp.float32)
        * score_scale
    ).astype(jnp.bfloat16)
    key_part = (
        jnp.einsum("qhisj,qihd->qsjd", grad_s, q_blocks, preferred_element_type=jnp.float32)
        * score_scale
    )
    value_part = jnp.einsum(
        "qhisj,qihd->qsjd",
        probability.astype(jnp.bfloat16),
        g_blocks,
        preferred_element_type=jnp.float32,
    )
    grad_tiles = jnp.stack([key_part, value_part], axis=2)
    remote_grad = grad_tiles[:, 1:].astype(jnp.bfloat16).reshape(my_entries, head_count, part_rows, HD)
    back = head_exchange(jnp.transpose(remote_grad, (1, 0, 2, 3)), head_idx, head_count).reshape(
        entry_count, part_rows, HD
    )
    slot_entry = (
        jnp.full((total_slots + 1,), entry_count, jnp.int32)
        .at[slot_idx]
        .set(jnp.arange(entry_count, dtype=jnp.int32))[:total_slots]
    )
    back = jnp.concatenate([back, jnp.zeros((1, part_rows, HD), back.dtype)], axis=0)
    outgoing_part = back[slot_entry]
    returned = lax.all_to_all(
        outgoing_part.reshape(pair_count, capacity, part_rows, HD),
        "ctx",
        split_axis=0,
        concat_axis=0,
        tiled=True,
    )
    target = jnp.where(requested >= 0, requested, QB).reshape(-1)
    pick = (jnp.arange(QB, dtype=jnp.int32)[:, None] == target[None, :]).astype(returned.dtype)
    returned_sum = jnp.dot(
        pick, returned.reshape(total_slots, part_rows * HD), preferred_element_type=jnp.float32
    ).reshape(QB, part_rows, HD)
    routed = head_exchange(returned_sum.reshape(head_count, rows_here, part_rows, HD), head_idx, head_count)
    routed = jnp.transpose(routed, (1, 0, 2, 3)).reshape(rows_here, 2, BLK, HD)
    final = grad_tiles[:, 0] + routed
    out_rows = rows_here * BLK
    out_cols = heads_all * HD // head_count
    outputs_split = jnp.transpose(
        jnp.stack([attended, query_grad]).reshape(2, out_rows, head_count, out_cols), (2, 0, 1, 3)
    )
    outputs_rows = head_exchange(outputs_split, head_idx, head_count)
    return (
        outputs_rows[:, 0].reshape(head_count * out_rows, out_cols),
        outputs_rows[:, 1].reshape(head_count * out_rows, out_cols),
        final[:, 0].reshape(rows_here * BLK, HD).astype(jnp.bfloat16),
        final[:, 1].reshape(rows_here * BLK, HD).astype(jnp.bfloat16),
    )

def solution(mesh):
    return jax.shard_map(
        on_device,
        mesh=mesh,
        in_specs=(
            P("ctx", "head"),
            P("ctx", None),
            P("ctx", None),
            P("ctx", "head"),
            P("ctx", None),
        ),
        out_specs=(
            P("ctx", "head"),
            P("ctx", "head"),
            P(("ctx", "head"), None),
            P(("ctx", "head"), None),
        ),
        check_vma=False,
    )
```

```python
import math

import jax
import jax.numpy as jnp
from jax import lax
from jax.sharding import PartitionSpec as P

HD = 128
BLK = 128
SEL = 8
QB = 8


NEG_FILL = -1e30


def block_home(block, half_blocks, pair_count):
    stretch_idx = block // half_blocks
    early_side = stretch_idx < pair_count
    owner_dev = jnp.where(early_side, stretch_idx, 2 * pair_count - 1 - stretch_idx)
    local_blk = block % half_blocks + jnp.where(early_side, 0, half_blocks)
    return (owner_dev, local_blk)


def entry_slots(list_rows, half_blocks, pair_count):
    extras = list_rows[:, 1:].reshape(-1)
    usable = extras >= 0
    owner_dev, local_blk = block_home(jnp.maximum(extras, 0), half_blocks, pair_count)
    onehot_own = (
        (owner_dev[:, None] == jnp.arange(pair_count, dtype=jnp.int32)[None, :]) & usable[:, None]
    ).astype(jnp.int32)
    running = jnp.cumsum(onehot_own, axis=0)
    rank_in = jnp.sum(onehot_own * running, axis=1) - 1
    return (owner_dev, local_blk, rank_in, usable)


def head_exchange(x, head_idx, count):
    ahead = x[(head_idx + jnp.arange(count, dtype=jnp.int32)) % count]
    got = [ahead[0]]
    for k in range(1, count):
        got.append(lax.ppermute(ahead[k], "head", [(j, (j + k) % count) for j in range(count)]))
    order = (head_idx - jnp.arange(count, dtype=jnp.int32)) % count
    return jnp.stack(got)[order]


def on_device(queries, key_rows, value_rows, out_grad, block_lists):
    pair_count = lax.axis_size("ctx")
    head_count = lax.axis_size("head")
    half_blocks = QB // 2
    capacity = (QB * (SEL - 1) + pair_count - 2) // (pair_count - 1)
    total_slots = pair_count * capacity
    device = lax.axis_index("ctx")
    head_idx = lax.axis_index("head")
    score_scale = 1.0 / math.sqrt(HD)
    rows_here = QB // head_count
    extras = SEL - 1
    entry_count = QB * extras
    my_entries = rows_here * extras
    part_rows = 2 * BLK // head_count
    owner_dev, local_blk, rank_in, usable = entry_slots(block_lists, half_blocks, pair_count)
    slot_idx = jnp.where(usable, owner_dev * capacity + rank_in, total_slots)
    req_table = (
        jnp.full((total_slots + 1,), -1, jnp.int32).at[slot_idx].set(local_blk)[:total_slots]
    )
    requested = lax.all_to_all(
        req_table.reshape(pair_count, capacity), "ctx", split_axis=0, concat_axis=0, tiled=True
    )
    rows_in, cols_in = queries.shape
    inputs_split = jnp.stack(
        [
            queries.reshape(head_count, rows_in // head_count, cols_in),
            out_grad.reshape(head_count, rows_in // head_count, cols_in),
        ],
        axis=1,
    )
    inputs_rows = head_exchange(inputs_split, head_idx, head_count)
    inputs_rows = jnp.transpose(inputs_rows, (1, 2, 0, 3)).reshape(2, rows_in // head_count, head_count * cols_in)
    q_rows = inputs_rows[0]
    g_rows = inputs_rows[1]
    heads_all = q_rows.shape[1] // HD
    kv_blocks = jnp.stack([key_rows.reshape(QB, BLK, HD), value_rows.reshape(QB, BLK, HD)], axis=1)
    kv_parts = kv_blocks.reshape(QB, head_count, part_rows, HD)
    my_part = lax.dynamic_index_in_dim(kv_parts, head_idx, axis=1, keepdims=False)
    send_parts = my_part[jnp.maximum(requested, 0)]
    entry_slot = jnp.where(usable, slot_idx, 0).reshape(head_count, my_entries)
    chunk_rows = part_rows // 2
    got_chunks = []
    for chunk in range(2):
        sent = send_parts[:, :, chunk * chunk_rows : (chunk + 1) * chunk_rows]
        fetched_chunk = lax.all_to_all(sent, "ctx", split_axis=0, concat_axis=0, tiled=True).reshape(
            total_slots, chunk_rows, HD
        )
        got_chunks.append(head_exchange(fetched_chunk[entry_slot], head_idx, head_count))
    got = jnp.concatenate(got_chunks, axis=2)
    remote_kv = jnp.transpose(got, (1, 0, 2, 3)).reshape(rows_here, extras, 2, BLK, HD)
    first_row = head_idx * rows_here
    own_kv = lax.dynamic_slice_in_dim(kv_blocks, first_row, rows_here, axis=0)
    kv_tiles = jnp.concatenate([own_kv[:, None], remote_kv], axis=1)
    key_tile = kv_tiles[:, :, 0]
    value_tile = kv_tiles[:, :, 1]
    my_lists = lax.dynamic_slice_in_dim(block_lists, first_row, rows_here, axis=0)
    local_ids = first_row + jnp.arange(rows_here, dtype=jnp.int32)
    own_block = jnp.where(
        local_ids < half_blocks,
        device * half_blocks + local_ids,
        (2 * pair_count - 1 - device) * half_blocks + local_ids - half_blocks,
    )
    offsets = jnp.arange(BLK, dtype=jnp.int32)
    query_pos = own_block[:, None] * BLK + offsets[None, :]
    key_pos = jnp.maximum(my_lists, 0)[:, :, None] * BLK + offsets[None, None, :]
    visible = (my_lists >= 0)[:, None, :, None] & (
        key_pos[:, None, :, :] <= query_pos[:, :, None, None]
    )
    q_blocks = q_rows.reshape(rows_here, BLK, heads_all, HD)
    g_blocks = g_rows.reshape(rows_here, BLK, heads_all, HD)
    scores = (
        jnp.einsum("qihd,qsjd->qhisj", q_blocks, key_tile, preferred_element_type=jnp.float32)
        * score_scale
    )
    scores = jnp.where(visible[:, None], scores, NEG_FILL)
    row_max = jnp.max(scores, axis=(3, 4), keepdims=True)
    weights = jnp.exp(scores - row_max)
    row_total = jnp.sum(weights, axis=(3, 4), keepdims=True)
    summed = jnp.einsum(
        "qhisj,qsjd->qihd",
        weights.astype(jnp.bfloat16),
        value_tile,
        preferred_element_type=jnp.float32,
    )
    attended = (summed / jnp.transpose(row_total[..., 0, 0], (0, 2, 1))[..., None]).astype(
        jnp.bfloat16
    )
    log_total = row_max + jnp.log(row_total)
    probability = jnp.exp(scores - log_total)
    row_delta = jnp.sum(g_blocks.astype(jnp.float32) * attended.astype(jnp.float32), axis=3)
    grad_p = jnp.einsum(
        "qihd,qsjd->qhisj", g_blocks, value_tile, preferred_element_type=jnp.float32
    )
    grad_s = (probability * (grad_p - jnp.transpose(row_delta, (0, 2, 1))[..., None, None])).astype(
        jnp.bfloat16
    )
    query_grad = (
        jnp.einsum("qhisj,qsjd->qihd", grad_s, key_tile, preferred_element_type=jnp.float32)
        * score_scale
    ).astype(jnp.bfloat16)
    key_part = (
        jnp.einsum("qhisj,qihd->qsjd", grad_s, q_blocks, preferred_element_type=jnp.float32)
        * score_scale
    )
    value_part = jnp.einsum(
        "qhisj,qihd->qsjd",
        probability.astype(jnp.bfloat16),
        g_blocks,
        preferred_element_type=jnp.float32,
    )
    grad_tiles = jnp.stack([key_part, value_part], axis=2)
    remote_grad = grad_tiles[:, 1:].astype(jnp.bfloat16).reshape(my_entries, head_count, part_rows, HD)
    back = head_exchange(jnp.transpose(remote_grad, (1, 0, 2, 3)), head_idx, head_count).reshape(
        entry_count, part_rows, HD
    )
    slot_entry = (
        jnp.full((total_slots + 1,), entry_count, jnp.int32)
        .at[slot_idx]
        .set(jnp.arange(entry_count, dtype=jnp.int32))[:total_slots]
    )
    back = jnp.concatenate([back, jnp.zeros((1, part_rows, HD), back.dtype)], axis=0)
    outgoing_part = back[slot_entry]
    returned = lax.all_to_all(
        outgoing_part.reshape(pair_count, capacity, part_rows, HD),
        "ctx",
        split_axis=0,
        concat_axis=0,
        tiled=True,
    ).astype(jnp.float32)
    target = jnp.where(requested >= 0, requested, QB).reshape(-1)
    returned_sum = (
        jnp.zeros((QB + 1, part_rows, HD), jnp.float32)
        .at[target]
        .add(returned.reshape(-1, part_rows, HD))[:QB]
    )
    routed = lax.all_to_all(
        returned_sum.reshape(head_count, rows_here, part_rows, HD), "head", split_axis=0, concat_axis=0, tiled=True
    )
    routed = jnp.transpose(routed, (1, 0, 2, 3)).reshape(rows_here, 2, BLK, HD)
    final = grad_tiles[:, 0] + routed
    out_rows = rows_here * BLK
    out_cols = heads_all * HD // head_count
    outputs_split = jnp.transpose(
        jnp.stack([attended, query_grad]).reshape(2, out_rows, head_count, out_cols), (2, 0, 1, 3)
    )
    outputs_rows = head_exchange(outputs_split, head_idx, head_count)
    return (
        outputs_rows[:, 0].reshape(head_count * out_rows, out_cols),
        outputs_rows[:, 1].reshape(head_count * out_rows, out_cols),
        final[:, 0].reshape(rows_here * BLK, HD).astype(jnp.bfloat16),
        final[:, 1].reshape(rows_here * BLK, HD).astype(jnp.bfloat16),
    )

def solution(mesh):
    return jax.shard_map(
        on_device,
        mesh=mesh,
        in_specs=(
            P("ctx", "head"),
            P("ctx", None),
            P("ctx", None),
            P("ctx", "head"),
            P("ctx", None),
        ),
        out_specs=(
            P("ctx", "head"),
            P("ctx", "head"),
            P(("ctx", "head"), None),
            P(("ctx", "head"), None),
        ),
        check_vma=False,
    )
```

```python
import math

import jax
import jax.numpy as jnp
from jax import lax
from jax.sharding import PartitionSpec as P

HD = 128
BLK = 128
SEL = 8
QB = 8


NEG_FILL = -1e30


def block_home(block, half_blocks, pair_count):
    stretch_idx = block // half_blocks
    early_side = stretch_idx < pair_count
    owner_dev = jnp.where(early_side, stretch_idx, 2 * pair_count - 1 - stretch_idx)
    local_blk = block % half_blocks + jnp.where(early_side, 0, half_blocks)
    return (owner_dev, local_blk)


def entry_slots(list_rows, half_blocks, pair_count):
    extras = list_rows[:, 1:].reshape(-1)
    usable = extras >= 0
    owner_dev, local_blk = block_home(jnp.maximum(extras, 0), half_blocks, pair_count)
    onehot_own = (
        (owner_dev[:, None] == jnp.arange(pair_count, dtype=jnp.int32)[None, :]) & usable[:, None]
    ).astype(jnp.int32)
    running = jnp.cumsum(onehot_own, axis=0)
    rank_in = jnp.sum(onehot_own * running, axis=1) - 1
    return (owner_dev, local_blk, rank_in, usable)


def head_exchange(x, head_idx, count):
    ahead = x[(head_idx + jnp.arange(count, dtype=jnp.int32)) % count]
    got = [ahead[0]]
    for k in range(1, count):
        got.append(lax.ppermute(ahead[k], "head", [(j, (j + k) % count) for j in range(count)]))
    order = (head_idx - jnp.arange(count, dtype=jnp.int32)) % count
    return jnp.stack(got)[order]


def on_device(queries, key_rows, value_rows, out_grad, block_lists):
    pair_count = lax.axis_size("ctx")
    head_count = lax.axis_size("head")
    half_blocks = QB // 2
    capacity = (QB * (SEL - 1) + pair_count - 2) // (pair_count - 1)
    total_slots = pair_count * capacity
    device = lax.axis_index("ctx")
    head_idx = lax.axis_index("head")
    score_scale = 1.0 / math.sqrt(HD)
    rows_here = QB // head_count
    extras = SEL - 1
    entry_count = QB * extras
    my_entries = rows_here * extras
    part_rows = 2 * BLK // head_count
    owner_dev, local_blk, rank_in, usable = entry_slots(block_lists, half_blocks, pair_count)
    slot_idx = jnp.where(usable, owner_dev * capacity + rank_in, total_slots)
    req_table = (
        jnp.full((total_slots + 1,), -1, jnp.int32).at[slot_idx].set(local_blk)[:total_slots]
    )
    requested = lax.all_to_all(
        req_table.reshape(pair_count, capacity), "ctx", split_axis=0, concat_axis=0, tiled=True
    )
    rows_in, cols_in = queries.shape
    inputs_split = jnp.stack(
        [
            queries.reshape(head_count, rows_in // head_count, cols_in),
            out_grad.reshape(head_count, rows_in // head_count, cols_in),
        ],
        axis=1,
    )
    inputs_rows = head_exchange(inputs_split, head_idx, head_count)
    inputs_rows = jnp.transpose(inputs_rows, (1, 2, 0, 3)).reshape(2, rows_in // head_count, head_count * cols_in)
    q_rows = inputs_rows[0]
    g_rows = inputs_rows[1]
    heads_all = q_rows.shape[1] // HD
    kv_blocks = jnp.stack([key_rows.reshape(QB, BLK, HD), value_rows.reshape(QB, BLK, HD)], axis=1)
    kv_parts = kv_blocks.reshape(QB, head_count, part_rows, HD)
    my_part = lax.dynamic_index_in_dim(kv_parts, head_idx, axis=1, keepdims=False)
    send_parts = my_part[jnp.maximum(requested, 0)]
    fetched_part = lax.all_to_all(send_parts, "ctx", split_axis=0, concat_axis=0, tiled=True).reshape(
        total_slots, part_rows, HD
    )
    entry_slot = jnp.where(usable, slot_idx, 0).reshape(head_count, my_entries)
    share = fetched_part[entry_slot]
    got = head_exchange(share, head_idx, head_count)
    remote_kv = jnp.transpose(got, (1, 0, 2, 3)).reshape(rows_here, extras, 2, BLK, HD)
    first_row = head_idx * rows_here
    own_kv = lax.dynamic_slice_in_dim(kv_blocks, first_row, rows_here, axis=0)
    kv_tiles = jnp.concatenate([own_kv[:, None], remote_kv], axis=1)
    key_tile = kv_tiles[:, :, 0]
    value_tile = kv_tiles[:, :, 1]
    my_lists = lax.dynamic_slice_in_dim(block_lists, first_row, rows_here, axis=0)
    local_ids = first_row + jnp.arange(rows_here, dtype=jnp.int32)
    own_block = jnp.where(
        local_ids < half_blocks,
        device * half_blocks + local_ids,
        (2 * pair_count - 1 - device) * half_blocks + local_ids - half_blocks,
    )
    offsets = jnp.arange(BLK, dtype=jnp.int32)
    query_pos = own_block[:, None] * BLK + offsets[None, :]
    key_pos = jnp.maximum(my_lists, 0)[:, :, None] * BLK + offsets[None, None, :]
    visible = (my_lists >= 0)[:, None, :, None] & (
        key_pos[:, None, :, :] <= query_pos[:, :, None, None]
    )
    q_blocks = q_rows.reshape(rows_here, BLK, heads_all, HD)
    g_blocks = g_rows.reshape(rows_here, BLK, heads_all, HD)
    scores = (
        jnp.einsum("qihd,qsjd->qhisj", q_blocks, key_tile, preferred_element_type=jnp.float32)
        * score_scale
    )
    scores = jnp.where(visible[:, None], scores, NEG_FILL)
    row_max = jnp.max(scores, axis=(3, 4), keepdims=True)
    weights = jnp.exp(scores - row_max)
    row_total = jnp.sum(weights, axis=(3, 4), keepdims=True)
    summed = jnp.einsum(
        "qhisj,qsjd->qihd",
        weights.astype(jnp.bfloat16),
        value_tile,
        preferred_element_type=jnp.float32,
    )
    attended = (summed / jnp.transpose(row_total[..., 0, 0], (0, 2, 1))[..., None]).astype(
        jnp.bfloat16
    )
    probability = weights * (1.0 / row_total)
    row_delta = jnp.sum(g_blocks.astype(jnp.float32) * attended.astype(jnp.float32), axis=3)
    grad_p = jnp.einsum(
        "qihd,qsjd->qhisj", g_blocks, value_tile, preferred_element_type=jnp.float32
    )
    grad_s = (probability * (grad_p - jnp.transpose(row_delta, (0, 2, 1))[..., None, None])).astype(
        jnp.bfloat16
    )
    query_grad = (
        jnp.einsum("qhisj,qsjd->qihd", grad_s, key_tile, preferred_element_type=jnp.float32)
        * score_scale
    ).astype(jnp.bfloat16)
    key_part = (
        jnp.einsum("qhisj,qihd->qsjd", grad_s, q_blocks, preferred_element_type=jnp.float32)
        * score_scale
    )
    value_part = jnp.einsum(
        "qhisj,qihd->qsjd",
        probability.astype(jnp.bfloat16),
        g_blocks,
        preferred_element_type=jnp.float32,
    )
    grad_tiles = jnp.stack([key_part, value_part], axis=2)
    remote_grad = grad_tiles[:, 1:].astype(jnp.bfloat16).reshape(my_entries, head_count, part_rows, HD)
    back = head_exchange(jnp.transpose(remote_grad, (1, 0, 2, 3)), head_idx, head_count).reshape(
        entry_count, part_rows, HD
    )
    slot_entry = (
        jnp.full((total_slots + 1,), entry_count, jnp.int32)
        .at[slot_idx]
        .set(jnp.arange(entry_count, dtype=jnp.int32))[:total_slots]
    )
    back = jnp.concatenate([back, jnp.zeros((1, part_rows, HD), back.dtype)], axis=0)
    outgoing_part = back[slot_entry]
    returned = lax.all_to_all(
        outgoing_part.reshape(pair_count, capacity, part_rows, HD),
        "ctx",
        split_axis=0,
        concat_axis=0,
        tiled=True,
    ).astype(jnp.float32)
    target = jnp.where(requested >= 0, requested, QB).reshape(-1)
    returned_sum = (
        jnp.zeros((QB + 1, part_rows, HD), jnp.float32)
        .at[target]
        .add(returned.reshape(-1, part_rows, HD))[:QB]
    )
    routed = head_exchange(returned_sum.reshape(head_count, rows_here, part_rows, HD), head_idx, head_count)
    routed = jnp.transpose(routed, (1, 0, 2, 3)).reshape(rows_here, 2, BLK, HD)
    final = grad_tiles[:, 0] + routed
    out_rows = rows_here * BLK
    out_cols = heads_all * HD // head_count
    outputs_split = jnp.transpose(
        jnp.stack([attended, query_grad]).reshape(2, out_rows, head_count, out_cols), (2, 0, 1, 3)
    )
    outputs_rows = head_exchange(outputs_split, head_idx, head_count)
    return (
        outputs_rows[:, 0].reshape(head_count * out_rows, out_cols),
        outputs_rows[:, 1].reshape(head_count * out_rows, out_cols),
        final[:, 0].reshape(rows_here * BLK, HD).astype(jnp.bfloat16),
        final[:, 1].reshape(rows_here * BLK, HD).astype(jnp.bfloat16),
    )

def solution(mesh):
    return jax.shard_map(
        on_device,
        mesh=mesh,
        in_specs=(
            P("ctx", "head"),
            P("ctx", None),
            P("ctx", None),
            P("ctx", "head"),
            P("ctx", None),
        ),
        out_specs=(
            P("ctx", "head"),
            P("ctx", "head"),
            P(("ctx", "head"), None),
            P(("ctx", "head"), None),
        ),
        check_vma=False,
    )
```

```python
import math

import jax
import jax.numpy as jnp
from jax import lax
from jax.sharding import PartitionSpec as P

HD = 128
BLK = 128
SEL = 8
QB = 8


NEG_FILL = -1e30


def block_home(block, half_blocks, pair_count):
    stretch_idx = block // half_blocks
    early_side = stretch_idx < pair_count
    owner_dev = jnp.where(early_side, stretch_idx, 2 * pair_count - 1 - stretch_idx)
    local_blk = block % half_blocks + jnp.where(early_side, 0, half_blocks)
    return (owner_dev, local_blk)


def entry_slots(list_rows, half_blocks, pair_count):
    extras = list_rows[:, 1:].reshape(-1)
    usable = extras >= 0
    owner_dev, local_blk = block_home(jnp.maximum(extras, 0), half_blocks, pair_count)
    onehot_own = (
        (owner_dev[:, None] == jnp.arange(pair_count, dtype=jnp.int32)[None, :]) & usable[:, None]
    ).astype(jnp.int32)
    running = jnp.cumsum(onehot_own, axis=0)
    rank_in = jnp.sum(onehot_own * running, axis=1) - 1
    return (owner_dev, local_blk, rank_in, usable)


def head_exchange(x, head_idx, count, reorder=True):
    ahead = x[(head_idx + jnp.arange(count, dtype=jnp.int32)) % count]
    got = [ahead[0]]
    for k in range(1, count):
        got.append(lax.ppermute(ahead[k], "head", [(j, (j + k) % count) for j in range(count)]))
    if not reorder:
        return jnp.stack(got)
    order = (head_idx - jnp.arange(count, dtype=jnp.int32)) % count
    return jnp.stack(got)[order]


def on_device(queries, key_rows, value_rows, out_grad, block_lists):
    pair_count = lax.axis_size("ctx")
    head_count = lax.axis_size("head")
    half_blocks = QB // 2
    capacity = (QB * (SEL - 1) + pair_count - 2) // (pair_count - 1)
    total_slots = pair_count * capacity
    device = lax.axis_index("ctx")
    head_idx = lax.axis_index("head")
    score_scale = 1.0 / math.sqrt(HD)
    rows_here = QB // head_count
    extras = SEL - 1
    entry_count = QB * extras
    my_entries = rows_here * extras
    part_rows = 2 * BLK // head_count
    owner_dev, local_blk, rank_in, usable = entry_slots(block_lists, half_blocks, pair_count)
    slot_idx = jnp.where(usable, owner_dev * capacity + rank_in, total_slots)
    req_table = (
        jnp.full((total_slots + 1,), -1, jnp.int32).at[slot_idx].set(local_blk)[:total_slots]
    )
    requested = lax.all_to_all(
        req_table.reshape(pair_count, capacity), "ctx", split_axis=0, concat_axis=0, tiled=True
    )
    rows_in, cols_in = queries.shape
    inputs_split = jnp.stack(
        [
            queries.reshape(head_count, rows_in // head_count, cols_in),
            out_grad.reshape(head_count, rows_in // head_count, cols_in),
        ],
        axis=1,
    )
    inputs_rows = head_exchange(inputs_split, head_idx, head_count)
    inputs_rows = jnp.transpose(inputs_rows, (1, 2, 0, 3)).reshape(2, rows_in // head_count, head_count * cols_in)
    q_rows = inputs_rows[0]
    g_rows = inputs_rows[1]
    heads_all = q_rows.shape[1] // HD
    kv_blocks = jnp.stack([key_rows.reshape(QB, BLK, HD), value_rows.reshape(QB, BLK, HD)], axis=1)
    kv_parts = kv_blocks.reshape(QB, head_count, part_rows, HD)
    my_part = lax.dynamic_index_in_dim(kv_parts, head_idx, axis=1, keepdims=False)
    send_parts = my_part[jnp.maximum(requested, 0)]
    fetched_part = lax.all_to_all(send_parts, "ctx", split_axis=0, concat_axis=0, tiled=True).reshape(
        total_slots, part_rows, HD
    )
    entry_slot = jnp.where(usable, slot_idx, 0).reshape(head_count, my_entries)
    share = fetched_part[entry_slot]
    got = head_exchange(share, head_idx, head_count)
    remote_kv = jnp.transpose(got, (1, 0, 2, 3)).reshape(rows_here, extras, 2, BLK, HD)
    first_row = head_idx * rows_here
    own_kv = lax.dynamic_slice_in_dim(kv_blocks, first_row, rows_here, axis=0)
    kv_tiles = jnp.concatenate([own_kv[:, None], remote_kv], axis=1)
    key_tile = kv_tiles[:, :, 0]
    value_tile = kv_tiles[:, :, 1]
    my_lists = lax.dynamic_slice_in_dim(block_lists, first_row, rows_here, axis=0)
    local_ids = first_row + jnp.arange(rows_here, dtype=jnp.int32)
    own_block = jnp.where(
        local_ids < half_blocks,
        device * half_blocks + local_ids,
        (2 * pair_count - 1 - device) * half_blocks + local_ids - half_blocks,
    )
    offsets = jnp.arange(BLK, dtype=jnp.int32)
    query_pos = own_block[:, None] * BLK + offsets[None, :]
    key_pos = jnp.maximum(my_lists, 0)[:, :, None] * BLK + offsets[None, None, :]
    visible = (my_lists >= 0)[:, None, :, None] & (
        key_pos[:, None, :, :] <= query_pos[:, :, None, None]
    )
    q_blocks = q_rows.reshape(rows_here, BLK, heads_all, HD)
    g_blocks = g_rows.reshape(rows_here, BLK, heads_all, HD)
    scores = (
        jnp.einsum("qihd,qsjd->qhisj", q_blocks, key_tile, preferred_element_type=jnp.float32)
        * score_scale
    )
    scores = jnp.where(visible[:, None], scores, NEG_FILL)
    row_max = jnp.max(scores, axis=(3, 4), keepdims=True)
    weights = jnp.exp(scores - row_max)
    row_total = jnp.sum(weights, axis=(3, 4), keepdims=True)
    summed = jnp.einsum(
        "qhisj,qsjd->qihd",
        weights.astype(jnp.bfloat16),
        value_tile,
        preferred_element_type=jnp.float32,
    )
    attended = (summed / jnp.transpose(row_total[..., 0, 0], (0, 2, 1))[..., None]).astype(
        jnp.bfloat16
    )
    log_total = row_max + jnp.log(row_total)
    probability = jnp.exp(scores - log_total)
    row_delta = jnp.sum(g_blocks.astype(jnp.float32) * attended.astype(jnp.float32), axis=3)
    grad_p = jnp.einsum(
        "qihd,qsjd->qhisj", g_blocks, value_tile, preferred_element_type=jnp.float32
    )
    grad_s = (probability * (grad_p - jnp.transpose(row_delta, (0, 2, 1))[..., None, None])).astype(
        jnp.bfloat16
    )
    query_grad = (
        jnp.einsum("qhisj,qsjd->qihd", grad_s, key_tile, preferred_element_type=jnp.float32)
        * score_scale
    ).astype(jnp.bfloat16)
    key_part = (
        jnp.einsum("qhisj,qihd->qsjd", grad_s, q_blocks, preferred_element_type=jnp.float32)
        * score_scale
    )
    value_part = jnp.einsum(
        "qhisj,qihd->qsjd",
        probability.astype(jnp.bfloat16),
        g_blocks,
        preferred_element_type=jnp.float32,
    )
    grad_tiles = jnp.stack([key_part, value_part], axis=2)
    remote_grad = grad_tiles[:, 1:].astype(jnp.bfloat16).reshape(my_entries, head_count, part_rows, HD)
    back = head_exchange(jnp.transpose(remote_grad, (1, 0, 2, 3)), head_idx, head_count, False).reshape(
        entry_count, part_rows, HD
    )
    slot_entry = (
        jnp.full((total_slots + 1,), entry_count, jnp.int32)
        .at[slot_idx]
        .set(jnp.arange(entry_count, dtype=jnp.int32))[:total_slots]
    )
    back = jnp.concatenate([back, jnp.zeros((1, part_rows, HD), back.dtype)], axis=0)
    source_group = slot_entry // my_entries
    by_shift = ((head_idx - source_group) % head_count) * my_entries + slot_entry % my_entries
    outgoing_part = back[jnp.where(slot_entry < entry_count, by_shift, entry_count)]
    returned = lax.all_to_all(
        outgoing_part.reshape(pair_count, capacity, part_rows, HD),
        "ctx",
        split_axis=0,
        concat_axis=0,
        tiled=True,
    ).astype(jnp.float32)
    target = jnp.where(requested >= 0, requested, QB).reshape(-1)
    returned_sum = (
        jnp.zeros((QB + 1, part_rows, HD), jnp.float32)
        .at[target]
        .add(returned.reshape(-1, part_rows, HD))[:QB]
    )
    routed = head_exchange(returned_sum.reshape(head_count, rows_here, part_rows, HD), head_idx, head_count)
    routed = jnp.transpose(routed, (1, 0, 2, 3)).reshape(rows_here, 2, BLK, HD)
    final = grad_tiles[:, 0] + routed
    out_rows = rows_here * BLK
    out_cols = heads_all * HD // head_count
    outputs_split = jnp.transpose(
        jnp.stack([attended, query_grad]).reshape(2, out_rows, head_count, out_cols), (2, 0, 1, 3)
    )
    outputs_rows = head_exchange(outputs_split, head_idx, head_count)
    return (
        outputs_rows[:, 0].reshape(head_count * out_rows, out_cols),
        outputs_rows[:, 1].reshape(head_count * out_rows, out_cols),
        final[:, 0].reshape(rows_here * BLK, HD).astype(jnp.bfloat16),
        final[:, 1].reshape(rows_here * BLK, HD).astype(jnp.bfloat16),
    )

def solution(mesh):
    return jax.shard_map(
        on_device,
        mesh=mesh,
        in_specs=(
            P("ctx", "head"),
            P("ctx", None),
            P("ctx", None),
            P("ctx", "head"),
            P("ctx", None),
        ),
        out_specs=(
            P("ctx", "head"),
            P("ctx", "head"),
            P(("ctx", "head"), None),
            P(("ctx", "head"), None),
        ),
        check_vma=False,
    )
```
